32 devices in a mesh: seq: 16 (over z, y, x), head: 2 (over core).
Axes of the slice: x: 2, y: 2, z: 4, core: 2. Of those that a mesh axis runs over, the one named last changes fastest.
Arguments:
- queries: bfloat16 [6144, 2048], P('seq', 'head'), may hold values from -6 to 6
- keys: bfloat16 [6144, 2048], P('seq', 'head'), may hold values from -0.5 to 0.5
- values: bfloat16 [6144, 2048], P('seq', 'head'), may hold values from -6 to 6
- level_pattern: int32 [6144], P('seq'), may hold values from 0 to 15
- level_weight: float32 [16, 9], replicated, may hold values from 0.5 to 2
- out_weight: bfloat16 [2, 1024, 2048], P('head', 'seq'), may hold values from -0.125 to 0.125
Outputs:
- mixed: float32 [6144, 2048], P('seq', 'head')
The draws below stay inside these ranges and needn't reach their ends.
All inputs are finite; a program needn't handle non-finite values.
Results may differ from the reference program's by a relative error of at most 0.003.
Values may be sent and summed in bfloat16 or wider, within the bound.
A program may use at most 64 MiB of HBM per device.

```python
import math
import jax
import jax.numpy as jnp
from jax import lax

D = 2048
HEADS = 16
HD = 128
LEVELS = 8
PATTERNS = 16
TOK_DEV = 384
TOKENS = 6144
N_SEQ = 16
N_HEAD = 2


def with_ends(result, stream_key, low, high):
    extent = result.shape
    index_at = [jax.random.randint(jax.random.fold_in(stream_key, axis), (), 0, extent[axis]) for axis in range(len(extent))]
    result = result.at[tuple(index_at)].set(low)
    longest = extent.index(max(extent))
    index_at[longest] = (index_at[longest] + 1) % extent[longest]
    return result.at[tuple(index_at)].set(high)


def levels(rng, shape, cuts, least, high):
    def one(position, shards_of):
        heights = jax.random.uniform(jax.random.fold_in(jax.random.fold_in(rng, 6), position), (shards_of,), jnp.float32, least / len(cuts), high / len(cuts))
        return jnp.repeat(jnp.exp(heights), shape[position] // shards_of).reshape((-1,) + (1,) * (len(shape) - position - 1))

    factor_of = one(*cuts[0])
    for cut in cuts[1:]:
        factor_of = factor_of * one(*cut)
    return factor_of


def centred(key, dims, deviation, limit, cuts=(), held_as=jnp.bfloat16):
    level = levels(key, dims, cuts, -0.22, 0.18) if cuts else 1.0
    drawn = jax.random.normal(key, dims, jnp.float32) * deviation * level
    return jnp.minimum(jnp.maximum(drawn, -limit), limit).astype(held_as)


def setup_inputs(seed: int = 0) -> dict:
    key_list = jax.random.split(jax.random.key(seed), 7)
    return {
        "queries": centred(key_list[0], (TOKENS, HEADS * HD), 1.0, 6.0, ((0, 16), (1, 2))),
        "keys": centred(key_list[1], (TOKENS, HEADS * HD), HD ** -0.5, 0.5, ((0, 16), (1, 2))),
        "values": centred(key_list[2], (TOKENS, HEADS * HD), 1.0, 6.0, ((0, 16), (1, 2))),
        "level_pattern": with_ends(jax.random.randint(key_list[3], (TOKENS,), 0, PATTERNS), jax.random.fold_in(key_list[3], 1), 0, PATTERNS - 1).astype(jnp.int32),
        "level_weight": jnp.clip(jnp.exp(jax.random.uniform(key_list[4], (PATTERNS, LEVELS + 1), jnp.float32, math.log(0.5), math.log(2.0))), 0.5, 2.0),
        "out_weight": centred(key_list[5], (N_HEAD, HEADS * HD // N_HEAD, D), (HEADS * HD) ** -0.5, 0.125, ((0, 2), (1, 16))),
    }


def reference(queries, keys, values, level_pattern, level_weight, out_weight):
    highest = lax.Precision.HIGHEST
    query = queries.reshape(N_SEQ, TOK_DEV, HEADS, HD).astype(jnp.float32)
    key_mat = keys.reshape(N_SEQ, TOK_DEV, HEADS, HD).astype(jnp.float32)
    value_mat = values.reshape(N_SEQ, TOK_DEV, HEADS, HD).astype(jnp.float32)
    scores = jnp.einsum('cthe,cshe->chts', query, key_mat, precision=highest)
    row_pos = lax.broadcasted_iota(jnp.int32, (TOK_DEV, TOK_DEV), 0)
    col_pos = lax.broadcasted_iota(jnp.int32, (TOK_DEV, TOK_DEV), 1)
    inner = jnp.where((col_pos <= row_pos)[None, None], scores, 0.0).astype(jnp.bfloat16)
    within = jnp.einsum('chts,cshf->cthf', inner.astype(jnp.float32), value_mat, precision=highest)
    within = within * (1.0 / math.sqrt(TOK_DEV))
    level_mix = level_weight[level_pattern].reshape(N_SEQ, TOK_DEV, LEVELS + 1)
    attended = level_mix[:, :, 0, None, None] * within
    states = jnp.einsum('cshe,cshf->chef', key_mat, value_mat, precision=highest)
    stretch_ids = jnp.arange(N_SEQ, dtype=jnp.int32)
    for level in range(LEVELS):
        span = 2 ** level
        if 2 * span > N_SEQ:
            break
        blocks = states.reshape(N_SEQ // span, span, HEADS, HD, HD).sum(axis=1)
        partner = blocks[jnp.bitwise_xor(stretch_ids // span, 1).astype(jnp.int32)]
        active = (stretch_ids // span % 2 == 1).astype(jnp.float32)
        level_read = jnp.einsum('cthe,chef->cthf', query, partner, precision=highest)
        factor = 1.0 / math.sqrt(span * TOK_DEV)
        coef = level_mix[:, :, level + 1] * active[:, None] * factor
        attended = attended + coef[:, :, None, None] * level_read
    attended = attended.reshape(TOKENS, HEADS * HD).astype(jnp.bfloat16)
    projection = out_weight.reshape(HEADS * HD, D)
    return jnp.dot(attended, projection, preferred_element_type=jnp.float32)
```

```python
import functools
import itertools
import math

import jax
import jax.numpy as jnp
from jax import lax
from jax.experimental import pallas as pl
from jax.experimental.pallas import tpu as pltpu
from jax.sharding import PartitionSpec as P

HD = 128
MESH = pl.DeviceIdType.MESH


def line_dims(mesh):
    n = mesh.shape["seq"]
    devices = mesh.devices.reshape(n, -1)[:, 0]
    coords = [tuple(getattr(d, "coords", ())) for d in devices]
    dims = []
    if len(set(coords)) == n:
        for axis in range(len(coords[0])):
            seen = [c[axis] - coords[0][axis] for c in coords]
            length = max(seen) + 1
            if length > 1:
                dims.append((length, seen.index(1)))
    stride = 1
    for length, step in sorted(dims, key=lambda d: d[1]):
        if step != stride:
            break
        stride *= length
    if not dims or stride != n:
        dims = [(2, 1 << i) for i in range(n.bit_length() - 1)]
    return sorted(dims, key=lambda d: -d[1])


def nearest(k, p, n):
    m = jnp.minimum(p, n - 1 - p)
    sign = jnp.where(p == m, 1, -1)
    near = (k + 1) // 2 * (2 * (k % 2) - 1)
    if n == 2:
        return p + k * (1 - 2 * p)
    return jnp.where(k <= 2 * m, p + near, p + sign * (k - m))


def kernel(
    plan, q_hbm, k_hbm, v_hbm, pattern_ref, table_ref, w_hbm, *rest
):
    dims, orders, cuts, events, n, fused = plan
    if fused:
        out_ref, *rest = rest
    else:
        att_hbm, w_out_hbm, *rest = rest
    (q_ref, k_ref, v_ref, w_ref, wbuf, att, acc, sub, outgoing, incoming, mixb,
     load_sem, own_sem, pair_send, pair_recv, w_send, w_recv, s_send, s_recv, a_send, a_recv) = rest
    me = lax.axis_index("seq")
    core = lax.axis_index("head")
    other = 1 - core
    tokens, width = q_ref.shape
    heads = width // HD
    cols = wbuf.shape[-1]
    bits = n.bit_length() - 1
    groups = a_send.shape[0]
    per = heads // groups
    place = [me // stride % length for length, stride in dims]

    loads = [
        pltpu.make_async_copy(src, dst, load_sem.at[i])
        for i, (src, dst) in enumerate(((w_hbm, w_ref), (k_hbm, k_ref), (v_hbm, v_ref), (q_hbm, q_ref)))
    ]
    for load in loads:
        load.start()

    barrier = pltpu.get_barrier_semaphore()
    total = 1
    pl.semaphore_signal(barrier, inc=1, device_id=(me, other), device_id_type=MESH)
    for bit in range(bits):
        pl.semaphore_signal(barrier, inc=1, device_id=(me ^ (1 << bit), core), device_id_type=MESH)
        total += 1
    for (length, stride), p in zip(dims, place):
        if length == 2:
            continue
        for step in (-1, 1):
            there = jnp.logical_and(p + step >= 0, p + step < length)

            @pl.when(there)
            def _():
                pl.semaphore_signal(barrier, inc=1, device_id=(me + step * stride, core), device_id_type=MESH)

            total = total + there.astype(jnp.int32)

    for l in range(bits + 1):
        if l == 0:
            ids = lax.broadcasted_iota(jnp.int32, (table_ref.shape[0], tokens), 0)
            one_hot = (ids == pattern_ref[...].reshape(1, tokens)).astype(jnp.float32)
            mix = lax.dot_general(
                one_hot, table_ref[...], (((0,), (0,)), ((), ())),
                precision=lax.Precision.HIGHEST, preferred_element_type=jnp.float32,
            )
        factor = 1.0 / math.sqrt(tokens * (1 if l == 0 else 2 ** (l - 1)))
        mixb[l] = jnp.broadcast_to(mix[:, l : l + 1] * factor, (tokens, HD))

    def head_cols(h):
        return slice(h * HD, (h + 1) * HD)

    loads[1].wait()
    loads[2].wait()

    def make_states(h):
        state = lax.dot_general(
            k_ref[:, head_cols(h)], v_ref[:, head_cols(h)], (((0,), (0,)), ((), ())),
            preferred_element_type=jnp.float32,
        )
        sub[h] = state
        outgoing[0, h] = state.astype(jnp.bfloat16)

    for h in range(heads):
        make_states(h)
    loads[0].wait()
    pl.semaphore_wait(barrier, total)

    def pair_copy():
        return pltpu.make_async_remote_copy(
            src_ref=w_ref.at[0, :, pl.ds(pl.multiple_of(other * cols, 128), cols)],
            dst_ref=wbuf.at[core, me], send_sem=pair_send, recv_sem=pair_recv,
            device_id=(me, other), device_id_type=MESH,
        )

    def pair_landed():
        return pltpu.make_async_remote_copy(
            src_ref=w_ref.at[0, :, pl.ds(pl.multiple_of(other * cols, 128), cols)],
            dst_ref=wbuf.at[other, me], send_sem=pair_send, recv_sem=pair_recv,
            device_id=(me, other), device_id_type=MESH,
        )

    pair_copy().start()
    own = pltpu.make_async_copy(
        w_ref.at[0, :, pl.ds(pl.multiple_of(core * cols, 128), cols)], wbuf.at[core, me], own_sem
    )
    own.start()

    def state_copy(level, group):
        piece = pl.ds(group * per, per)
        return pltpu.make_async_remote_copy(
            src_ref=outgoing.at[level, piece], dst_ref=incoming.at[level, piece],
            send_sem=s_send.at[level, group], recv_sem=s_recv.at[level, group],
            device_id=(me ^ (1 << level), core), device_id_type=MESH,
        )

    def sum_needed(level):
        return me // 2 ** (level + 1) != n // 2 ** (level + 1) - 1

    def active(level):
        return me // 2**level % 2 == 1

    def sends(level):
        return jnp.logical_or(jnp.logical_not(active(level)), sum_needed(level))

    def receives(level):
        return jnp.logical_or(active(level), sum_needed(level))

    for group in range(groups):
        @pl.when(sends(0))
        def _():
            state_copy(0, group).start()

    def weight_copy(part, source, slot, target):
        lo, size = cuts[part]
        piece = wbuf.at[:, source, :, pl.ds(lo, size)]
        return pltpu.make_async_remote_copy(
            src_ref=piece, dst_ref=piece,
            send_sem=w_send.at[part, source if fused else 0, slot], recv_sem=w_recv.at[part, source],
            device_id=(target, core), device_id_type=MESH,
        )

    def forward(part, source, at, arrived, action):
        order = orders[part]
        for rank in range(max(arrived, 0), len(order)):
            d = order[rank]
            length, stride = dims[d]
            for slot, step in ((2 * rank, 1), (2 * rank + 1, -1)):
                if rank == arrived and length == 2:
                    continue
                ok = jnp.logical_and(place[d] + step >= 0, place[d] + step < length)
                if rank == arrived:
                    ok = jnp.logical_and(ok, (place[d] - at[d]) * step > 0)

                @pl.when(ok)
                def _():
                    copy = weight_copy(part, source, slot, me + step * stride)
                    if action == "start":
                        copy.start()
                    else:
                        copy.wait_send()

    def source_of(part, ks):
        at = {d: nearest(k, place[d], dims[d][0]) for d, k in zip(orders[part], ks)}
        return at, sum(at[d] * dims[d][1] for d in at)

    def arrived_by(ks):
        return max((r for r, k in enumerate(ks) if k), default=-1)

    def weight_event(part, ks, arrived):
        at, source = source_of(part, ks)
        weight_copy(part, source, 0, me).wait_recv()
        forward(part, source, at, arrived, "start")
        if not fused:
            forward(part, source, at, arrived, "wait")

    def read_state(level, h):
        acc[:, head_cols(h)] += mixb[level + 1] * jnp.dot(
            q_ref[:, head_cols(h)], incoming[level, h], preferred_element_type=jnp.float32
        )

    def within_event(h):
        columns = head_cols(h)
        scores = lax.dot_general(
            q_ref[:, columns], k_ref[:, columns], (((1,), (1,)), ((), ())),
            preferred_element_type=jnp.float32,
        )
        row = lax.broadcasted_iota(jnp.int32, (tokens, tokens), 0)
        col = lax.broadcasted_iota(jnp.int32, (tokens, tokens), 1)
        inner = jnp.where(col <= row, scores, 0.0).astype(jnp.bfloat16)
        acc[:, columns] = mixb[0] * jnp.dot(inner, v_ref[:, columns], preferred_element_type=jnp.float32)

    def att_copy(group, mine):
        columns = pl.ds(group * per * HD, per * HD)
        which = core if mine else other
        return pltpu.make_async_remote_copy(
            src_ref=att.at[core, :, columns], dst_ref=att.at[which, :, columns],
            send_sem=a_send.at[group], recv_sem=a_recv.at[group],
            device_id=(me, other), device_id_type=MESH,
        )

    def state_event(level, group):
        @pl.when(receives(level))
        def _():
            state_copy(level, group).wait_recv()

        span = range(group * per, (group + 1) * per)
        if level + 1 < bits:
            @pl.when(sum_needed(level))
            def _():
                for h in span:
                    summed = sub[h] + incoming[level, h].astype(jnp.float32)
                    sub[h] = summed
                    outgoing[level + 1, h] = summed.astype(jnp.bfloat16)

            @pl.when(sends(level + 1))
            def _():
                state_copy(level + 1, group).start()

        @pl.when(active(level))
        def _():
            for h in span:
                read_state(level, h)

        if level + 1 == bits:
            columns = slice(group * per * HD, (group + 1) * per * HD)
            att[core, :, columns] = acc[:, columns].astype(jnp.bfloat16)
            att_copy(group, True).start()

    own.wait()
    pair_landed().wait_recv()
    for part in range(len(orders)):
        at, source = source_of(part, (0,) * len(dims))
        forward(part, source, at, -1, "start")
        if not fused:
            forward(part, source, at, -1, "wait")
    loads[3].wait()

    def project(part):
        lo, size = cuts[part]
        columns = slice(lo, lo + size)
        flat = [wbuf[g, :, :, columns].reshape(-1, size) for g in range(2)]
        out_ref[:, columns] = jnp.dot(att[0], flat[0], preferred_element_type=jnp.float32) + jnp.dot(
            att[1], flat[1], preferred_element_type=jnp.float32
        )

    for event in events:
        if event[0] == "within":
            within_event(event[1])
        elif event[0] == "state":
            state_event(event[1], event[2])
        elif event[0] == "weight":
            weight_event(*event[1:])
        elif event[0] == "loop":
            lengths = [[dims[d][0] for d in order] for order in orders]

            def each(e, carry):
                for part, order in enumerate(orders):
                    for arrived in range(len(order)):
                        below = math.prod(lengths[part][:arrived])
                        ks = []
                        rest_e = e
                        for length in lengths[part]:
                            ks.append(rest_e % length)
                            rest_e = rest_e // length

                        @pl.when(jnp.logical_and(e >= below, e < below * lengths[part][arrived]))
                        def _():
                            weight_event(part, ks, arrived)

                return carry

            lax.fori_loop(1, n, each, 0)
        elif event[0] == "att":
            for group in range(groups):
                att_copy(group, False).wait_recv()
        elif event[0] == "project" and fused:
            project(event[1])

    def finish(part, e):
        ks = []
        for d in orders[part]:
            ks.append(e % dims[d][0])
            e = e // dims[d][0]
        return ks

    pair_copy().wait_send()
    for group in range(groups):
        att_copy(group, True).wait_send()
        for level in range(bits):
            @pl.when(sends(level))
            def _():
                state_copy(level, group).wait_send()
    if fused:
        for part in range(len(orders)):
            for e in range(n):
                ks = finish(part, e)
                at, source = source_of(part, ks)
                forward(part, source, at, arrived_by(ks), "wait")
    if not fused:
        stores = [pltpu.make_async_copy(att, att_hbm, load_sem.at[0]), pltpu.make_async_copy(wbuf, w_out_hbm, load_sem.at[1])]
        for store in stores:
            store.start()
        for store in stores:
            store.wait()


def schedule(dims, orders, cuts, n, heads, groups, unrolled):
    bits = n.bit_length() - 1
    whole = sum(size for _, size in cuts)
    timed = []
    for h in range(heads):
        timed.append((0.35 * h / heads, ("within", h)))
    for level in range(bits):
        for group in range(groups):
            timed.append((0.45 + 0.75 * level + 0.25 * group, ("state", level, group)))
    if not unrolled:
        tail = [("loop",), ("att",)]
    else:
        last = {}
        for part, order in enumerate(orders):
            lengths = [dims[d][0] for d in order]
            count = [0] * len(order)
            for rev in itertools.product(*[range(length) for length in lengths[::-1]]):
                ks = rev[::-1]
                arrived = max((r for r, k in enumerate(ks) if k), default=-1)
                if arrived < 0:
                    continue
                count[arrived] += 1
                when = count[arrived] * cuts[part][1] / whole * 1.8 + 0.3 * sum(1 for k in ks if k)
                if arrived == len(order) - 1 and lengths[-1] == 2:
                    when += 100
                timed.append((when, ("weight", part, ks, arrived)))
        tail = [("att",)]
    timed.sort(key=lambda t: t[0])
    return [e for _, e in timed] + tail + [("project", p) for p in range(len(orders))]


def on_device(dims, queries, keys, values, level_pattern, level_weight, out_weight):
    n = lax.axis_size("seq")
    tokens, width = queries.shape
    heads = width // HD
    bits = n.bit_length() - 1
    _, rows, full = out_weight.shape
    cols = full // 2
    fused = rows % 16 == 0
    groups = min(4, heads)
    tiles = cols // 128
    if len(dims) == 3:
        long = max(range(3), key=lambda i: dims[i][0])
        a, b = [i for i in range(3) if i != long]
        orders = [(long, a, b), (long, b, a), (a, b, long)]
        share = max(1, tiles * 3 // 8)
        sizes = [share, share, tiles - 2 * share]
    else:
        orders, sizes = [tuple(range(len(dims)))], [tiles]
    cuts, lo = [], 0
    for size in sizes:
        cuts.append((lo * 128, size * 128))
        lo += size
    events = schedule(dims, orders, cuts, n, heads, groups, fused)
    plan = (dims, orders, cuts, events, n, fused)
    bf16, f32 = jnp.bfloat16, jnp.float32
    any_spec = pl.BlockSpec(memory_space=pl.ANY)
    vmem_spec = pl.BlockSpec(memory_space=pltpu.VMEM)
    if fused:
        out_shape = pltpu.VMEM((tokens, cols), f32)
        out_specs = vmem_spec
    else:
        out_shape = [
            jax.ShapeDtypeStruct((2, tokens, width), bf16),
            jax.ShapeDtypeStruct((2, n, rows, cols), bf16),
        ]
        out_specs = [any_spec, any_spec]
    dma = pltpu.SemaphoreType.DMA
    result = pl.pallas_call(
        functools.partial(kernel, plan),
        out_shape=out_shape,
        in_specs=[any_spec] * 3 + [vmem_spec] * 2 + [any_spec],
        out_specs=out_specs,
        scratch_shapes=[
            pltpu.VMEM((tokens, width), bf16),
            pltpu.VMEM((tokens, width), bf16),
            pltpu.VMEM((tokens, width), bf16),
            pltpu.VMEM((1, rows, full), bf16),
            pltpu.VMEM((2, n, rows, cols), bf16),
            pltpu.VMEM((2, tokens, width), bf16),
            pltpu.VMEM((tokens, width), f32),
            pltpu.VMEM((heads, HD, HD), f32),
            pltpu.VMEM((bits, heads, HD, HD), bf16),
            pltpu.VMEM((bits, heads, HD, HD), bf16),
            pltpu.VMEM((bits + 1, tokens, HD), f32),
            dma((4,)),
            dma,
            dma,
            dma,
            dma((len(orders), n if fused else 1, 2 * len(dims))),
            dma((len(orders), n)),
            dma((bits, groups)),
            dma((bits, groups)),
            dma((groups,)),
            dma((groups,)),
        ],
        compiler_params=pltpu.CompilerParams(
            collective_id=0, has_side_effects=True, vmem_limit_bytes=60 * 2**20
        ),
    )(queries, keys, values, level_pattern, level_weight, out_weight)
    if fused:
        return result
    att, gathered = result
    return jnp.einsum(
        "gtk,gkd->td", att, gathered.reshape(2, n * rows, cols), preferred_element_type=f32
    )


def solution(mesh):
    placed = (
        P("seq", "head"),
        P("seq", "head"),
        P("seq", "head"),
        P("seq"),
        P(),
        P("head", "seq", None),
    )
    return jax.shard_map(
        functools.partial(on_device, line_dims(mesh)),
        mesh=mesh, in_specs=placed, out_specs=P("seq", "head"), check_vma=False,
    )
```

```python
import functools
import itertools
import math

import jax
import jax.numpy as jnp
from jax import lax
from jax.experimental import pallas as pl
from jax.experimental.pallas import tpu as pltpu
from jax.sharding import PartitionSpec as P

HD = 128
MESH = pl.DeviceIdType.MESH
ORDER = (15, 0, 4, 16, 9, 10, 13, 18, 19, 22, 3, 20, 6, 8, 12, 7, 21, 17, 11, 30, 2, 14, 64, 31, 94, 53, 29, 5, 32, 49, 1, 92, 79, 113, 122, 109, 121, 68, 34, 25, 123, 128, 33, 46, 98, 35, 61, 66, 107, 80, 62, 36, 95, 83, 77, 124, 38, 24, 47, 28, 57, 76, 40, 106, 51, 93, 65, 39, 26, 117, 72, 102, 111, 81, 129, 37, 132, 27, 44, 108, 42, 100, 87, 130, 125, 55, 23, 59, 84, 41, 115, 91, 43, 73, 69, 103, 45, 88, 70, 96, 134, 52, 114, 133, 131, 58, 82, 54, 104, 74, 101, 99, 89, 63, 135, 50, 90, 110, 119, 86, 85, 126, 56, 71, 67, 118, 127, 60, 48, 75, 97, 78, 116, 112, 120, 105,)
LENGTHS = [4, 2, 2]
LAG = 6


def line_dims(mesh):
    n = mesh.shape["seq"]
    devices = mesh.devices.reshape(n, -1)[:, 0]
    coords = [tuple(getattr(d, "coords", ())) for d in devices]
    dims = []
    if len(set(coords)) == n:
        for axis in range(len(coords[0])):
            seen = [c[axis] - coords[0][axis] for c in coords]
            length = max(seen) + 1
            if length > 1:
                dims.append((length, seen.index(1)))
    stride = 1
    for length, step in sorted(dims, key=lambda d: d[1]):
        if step != stride:
            break
        stride *= length
    if not dims or stride != n:
        dims = [(2, 1 << i) for i in range(n.bit_length() - 1)]
    return sorted(dims, key=lambda d: -d[1])


def nearest(k, p, n):
    m = jnp.minimum(p, n - 1 - p)
    sign = jnp.where(p == m, 1, -1)
    near = (k + 1) // 2 * (2 * (k % 2) - 1)
    if n == 2:
        return p + k * (1 - 2 * p)
    return jnp.where(k <= 2 * m, p + near, p + sign * (k - m))


def kernel(
    plan, q_hbm, k_hbm, v_hbm, pattern_ref, table_ref, w_hbm, *rest
):
    dims, orders, cuts, events, n, fused = plan
    if fused:
        out_ref, *rest = rest
    else:
        att_hbm, w_out_hbm, *rest = rest
    (q_ref, k_ref, v_ref, w_ref, wbuf, att, acc, sub, outgoing, incoming, mixb,
     load_sem, own_sem, pair_send, pair_recv, w_send, w_recv, s_send, s_recv, a_send, a_recv) = rest
    me = lax.axis_index("seq")
    core = lax.axis_index("head")
    other = 1 - core
    tokens, width = q_ref.shape
    heads = width // HD
    cols = wbuf.shape[-1]
    bits = n.bit_length() - 1
    groups = a_send.shape[0]
    per = heads // groups
    place = [me // stride % length for length, stride in dims]

    loads = [
        pltpu.make_async_copy(src, dst, load_sem.at[i])
        for i, (src, dst) in enumerate(((w_hbm, w_ref), (k_hbm, k_ref), (v_hbm, v_ref), (q_hbm, q_ref)))
    ]
    for load in loads:
        load.start()

    barrier = pltpu.get_barrier_semaphore()
    total = 1
    pl.semaphore_signal(barrier, inc=1, device_id=(me, other), device_id_type=MESH)
    for bit in range(bits):
        pl.semaphore_signal(barrier, inc=1, device_id=(me ^ (1 << bit), core), device_id_type=MESH)
        total += 1
    for (length, stride), p in zip(dims, place):
        if length == 2:
            continue
        for step in (-1, 1):
            there = jnp.logical_and(p + step >= 0, p + step < length)

            @pl.when(there)
            def _():
                pl.semaphore_signal(barrier, inc=1, device_id=(me + step * stride, core), device_id_type=MESH)

            total = total + there.astype(jnp.int32)

    for l in range(bits + 1):
        if l == 0:
            ids = lax.broadcasted_iota(jnp.int32, (table_ref.shape[0], tokens), 0)
            one_hot = (ids == pattern_ref[...].reshape(1, tokens)).astype(jnp.float32)
            mix = lax.dot_general(
                one_hot, table_ref[...], (((0,), (0,)), ((), ())),
                precision=lax.Precision.HIGHEST, preferred_element_type=jnp.float32,
            )
        factor = 1.0 / math.sqrt(tokens * (1 if l == 0 else 2 ** (l - 1)))
        mixb[l] = jnp.broadcast_to(mix[:, l : l + 1] * factor, (tokens, HD))

    def head_cols(h):
        return slice(h * HD, (h + 1) * HD)

    loads[1].wait()
    loads[2].wait()

    def make_states(h):
        state = lax.dot_general(
            k_ref[:, head_cols(h)], v_ref[:, head_cols(h)], (((0,), (0,)), ((), ())),
            preferred_element_type=jnp.float32,
        )
        sub[h] = state
        outgoing[0, h] = state.astype(jnp.bfloat16)

    for h in range(heads):
        make_states(h)
    loads[0].wait()
    pl.semaphore_wait(barrier, total)

    def pair_copy():
        return pltpu.make_async_remote_copy(
            src_ref=w_ref.at[0, :, pl.ds(pl.multiple_of(other * cols, 128), cols)],
            dst_ref=wbuf.at[core, me], send_sem=pair_send, recv_sem=pair_recv,
            device_id=(me, other), device_id_type=MESH,
        )

    def pair_landed():
        return pltpu.make_async_remote_copy(
            src_ref=w_ref.at[0, :, pl.ds(pl.multiple_of(other * cols, 128), cols)],
            dst_ref=wbuf.at[other, me], send_sem=pair_send, recv_sem=pair_recv,
            device_id=(me, other), device_id_type=MESH,
        )

    pair_copy().start()
    own = pltpu.make_async_copy(
        w_ref.at[0, :, pl.ds(pl.multiple_of(core * cols, 128), cols)], wbuf.at[core, me], own_sem
    )
    own.start()

    def state_copy(level, group):
        piece = pl.ds(group * per, per)
        return pltpu.make_async_remote_copy(
            src_ref=outgoing.at[level, piece], dst_ref=incoming.at[level, piece],
            send_sem=s_send.at[level, group], recv_sem=s_recv.at[level, group],
            device_id=(me ^ (1 << level), core), device_id_type=MESH,
        )

    def sum_needed(level):
        return me // 2 ** (level + 1) != n // 2 ** (level + 1) - 1

    def active(level):
        return me // 2**level % 2 == 1

    def sends(level):
        return jnp.logical_or(jnp.logical_not(active(level)), sum_needed(level))

    def receives(level):
        return jnp.logical_or(active(level), sum_needed(level))

    for group in range(groups):
        @pl.when(sends(0))
        def _():
            state_copy(0, group).start()

    def weight_copy(part, source, slot, target):
        lo, size = cuts[part]
        piece = wbuf.at[:, source, :, pl.ds(lo, size)]
        return pltpu.make_async_remote_copy(
            src_ref=piece, dst_ref=piece,
            send_sem=w_send.at[part, source if fused else 0, slot], recv_sem=w_recv.at[part, source],
            device_id=(target, core), device_id_type=MESH,
        )

    def forward(part, source, at, arrived, action):
        order = orders[part]
        for rank in range(max(arrived, 0), len(order)):
            d = order[rank]
            length, stride = dims[d]
            for slot, step in ((2 * rank, 1), (2 * rank + 1, -1)):
                if rank == arrived and length == 2:
                    continue
                ok = jnp.logical_and(place[d] + step >= 0, place[d] + step < length)
                if rank == arrived:
                    ok = jnp.logical_and(ok, (place[d] - at[d]) * step > 0)

                @pl.when(ok)
                def _():
                    copy = weight_copy(part, source, slot, me + step * stride)
                    if action == "start":
                        copy.start()
                    else:
                        copy.wait_send()

    def source_of(part, ks):
        at = {d: nearest(k, place[d], dims[d][0]) for d, k in zip(orders[part], ks)}
        return at, sum(at[d] * dims[d][1] for d in at)

    def arrived_by(ks):
        return max((r for r, k in enumerate(ks) if k), default=-1)

    def weight_event(part, ks, arrived):
        at, source = source_of(part, ks)
        weight_copy(part, source, 0, me).wait_recv()
        forward(part, source, at, arrived, "start")
        if not fused:
            forward(part, source, at, arrived, "wait")

    def read_state(level, h):
        acc[:, head_cols(h)] += mixb[level + 1] * jnp.dot(
            q_ref[:, head_cols(h)], incoming[level, h], preferred_element_type=jnp.float32
        )

    def within_event(h):
        columns = head_cols(h)
        scores = lax.dot_general(
            q_ref[:, columns], k_ref[:, columns], (((1,), (1,)), ((), ())),
            preferred_element_type=jnp.float32,
        )
        row = lax.broadcasted_iota(jnp.int32, (tokens, tokens), 0)
        col = lax.broadcasted_iota(jnp.int32, (tokens, tokens), 1)
        inner = jnp.where(col <= row, scores, 0.0).astype(jnp.bfloat16)
        acc[:, columns] = mixb[0] * jnp.dot(inner, v_ref[:, columns], preferred_element_type=jnp.float32)

    def att_copy(group, mine):
        columns = pl.ds(group * per * HD, per * HD)
        which = core if mine else other
        return pltpu.make_async_remote_copy(
            src_ref=att.at[core, :, columns], dst_ref=att.at[which, :, columns],
            send_sem=a_send.at[group], recv_sem=a_recv.at[group],
            device_id=(me, other), device_id_type=MESH,
        )

    def state_event(level, group):
        @pl.when(receives(level))
        def _():
            state_copy(level, group).wait_recv()

        span = range(group * per, (group + 1) * per)
        if level + 1 < bits:
            @pl.when(sum_needed(level))
            def _():
                for h in span:
                    summed = sub[h] + incoming[level, h].astype(jnp.float32)
                    sub[h] = summed
                    outgoing[level + 1, h] = summed.astype(jnp.bfloat16)

            @pl.when(sends(level + 1))
            def _():
                state_copy(level + 1, group).start()

        @pl.when(active(level))
        def _():
            for h in span:
                read_state(level, h)

        if level + 1 == bits:
            columns = slice(group * per * HD, (group + 1) * per * HD)
            att[core, :, columns] = acc[:, columns].astype(jnp.bfloat16)
            att_copy(group, True).start()

    own.wait()
    pair_landed().wait_recv()
    for part in range(len(orders)):
        at, source = source_of(part, (0,) * len(dims))
        forward(part, source, at, -1, "start")
        if not fused:
            forward(part, source, at, -1, "wait")
    loads[3].wait()

    def project(part):
        lo, size = cuts[part]
        columns = slice(lo, lo + size)
        flat = [wbuf[g, :, :, columns].reshape(-1, size) for g in range(2)]
        out_ref[:, columns] = jnp.dot(att[0], flat[0], preferred_element_type=jnp.float32) + jnp.dot(
            att[1], flat[1], preferred_element_type=jnp.float32
        )

    for event in events:
        if event[0] == "within":
            within_event(event[1])
        elif event[0] == "state":
            state_event(event[1], event[2])
        elif event[0] == "weight":
            weight_event(*event[1:])
        elif event[0] == "loop":
            lengths = [[dims[d][0] for d in order] for order in orders]

            def each(e, carry):
                for part, order in enumerate(orders):
                    for arrived in range(len(order)):
                        below = math.prod(lengths[part][:arrived])
                        ks = []
                        rest_e = e
                        for length in lengths[part]:
                            ks.append(rest_e % length)
                            rest_e = rest_e // length

                        @pl.when(jnp.logical_and(e >= below, e < below * lengths[part][arrived]))
                        def _():
                            weight_event(part, ks, arrived)

                return carry

            lax.fori_loop(1, n, each, 0)
        elif event[0] == "att":
            for group in range(groups):
                att_copy(group, False).wait_recv()
        elif event[0] == "project" and fused:
            project(event[1])

    def finish(part, e):
        ks = []
        for d in orders[part]:
            ks.append(e % dims[d][0])
            e = e // dims[d][0]
        return ks

    pair_copy().wait_send()
    for group in range(groups):
        att_copy(group, True).wait_send()
        for level in range(bits):
            @pl.when(sends(level))
            def _():
                state_copy(level, group).wait_send()
    if fused:
        for part in range(len(orders)):
            for e in range(n):
                ks = finish(part, e)
                at, source = source_of(part, ks)
                forward(part, source, at, arrived_by(ks), "wait")
    if not fused:
        stores = [pltpu.make_async_copy(att, att_hbm, load_sem.at[0]), pltpu.make_async_copy(wbuf, w_out_hbm, load_sem.at[1])]
        for store in stores:
            store.start()
        for store in stores:
            store.wait()


def schedule(dims, orders, cuts, n, heads, groups, unrolled):
    bits = n.bit_length() - 1
    whole = sum(size for _, size in cuts)
    timed = []
    for h in range(heads):
        timed.append((0.35 * h / heads, ("within", h)))
    for level in range(bits):
        for group in range(groups):
            timed.append((0.45 + 0.75 * level + 0.25 * group, ("state", level, group)))
    if not unrolled:
        tail = [("loop",), ("att",)]
    else:
        last = {}
        for part, order in enumerate(orders):
            lengths = [dims[d][0] for d in order]
            count = [0] * len(order)
            for rev in itertools.product(*[range(length) for length in lengths[::-1]]):
                ks = rev[::-1]
                arrived = max((r for r, k in enumerate(ks) if k), default=-1)
                if arrived < 0:
                    continue
                count[arrived] += 1
                when = count[arrived] * cuts[part][1] / whole * 1.8 + 0.3 * sum(1 for k in ks if k)
                if arrived == len(order) - 1 and lengths[-1] == 2:
                    when += 100
                timed.append((when, ("weight", part, ks, arrived)))
        tail = [("att",)]
    timed.sort(key=lambda t: t[0])
    return [e for _, e in timed] + tail + [("project", p) for p in range(len(orders))]


def planned_kernel(
    plan, q_hbm, k_hbm, v_hbm, pattern_ref, table_ref, w_hbm, out_ref,
    q_ref, k_ref, v_ref, w_ref, wbuf, att, acc, sub, outgoing, incoming, mixb,
    load_sem, own_sem, pair_send, pair_recv, w_send, w_recv, s_send, s_recv, a_send, a_recv,
):
    dims, parts, events, n = plan
    me = lax.axis_index("seq")
    core = lax.axis_index("head")
    other = 1 - core
    tokens, width = q_ref.shape
    rows = w_ref.shape[1]
    heads = width // HD
    cols = wbuf.shape[-1]
    bits = n.bit_length() - 1
    groups = s_recv.shape[1]
    per = heads // groups
    place = [me // stride % length for length, stride in dims]

    loads = {
        name: pltpu.make_async_copy(src, dst, load_sem.at[i])
        for i, (name, src, dst) in enumerate(
            (("w", w_hbm, w_ref), ("k", k_hbm, k_ref), ("v", v_hbm, v_ref), ("q", q_hbm, q_ref))
        )
    }
    for load in loads.values():
        load.start()

    barrier = pltpu.get_barrier_semaphore()
    total = 1
    pl.semaphore_signal(barrier, inc=1, device_id=(me, other), device_id_type=MESH)
    for (length, stride), p in zip(dims, place):
        for step in (-1, 1):
            there = jnp.logical_and(p + step >= 0, p + step < length)

            @pl.when(there)
            def _():
                for c in range(2):
                    pl.semaphore_signal(barrier, inc=1, device_id=(me + step * stride, c), device_id_type=MESH)

            total = total + 2 * there.astype(jnp.int32)
    for bit in range(bits):
        if all(1 << bit != stride for _, stride in dims):
            pl.semaphore_signal(barrier, inc=1, device_id=(me ^ (1 << bit), core), device_id_type=MESH)
            total = total + 1

    waited = set()

    def loaded(*names):
        for name in names:
            if name not in waited:
                waited.add(name)
                loads[name].wait()

    loaded("w")
    pl.semaphore_wait(barrier, total)

    def head_cols(h):
        return slice(h * HD, (h + 1) * HD)

    def pair_copy(which):
        return pltpu.make_async_remote_copy(
            src_ref=w_ref.at[0, :, pl.ds(pl.multiple_of(other * cols, 128), cols)],
            dst_ref=wbuf.at[which, me], send_sem=pair_send, recv_sem=pair_recv,
            device_id=(me, other), device_id_type=MESH,
        )

    own = pltpu.make_async_copy(
        w_ref.at[0, :, pl.ds(pl.multiple_of(core * cols, 128), cols)], wbuf.at[core, me], own_sem
    )

    def state_copy(level, group):
        piece = pl.ds(group * per, per)
        return pltpu.make_async_remote_copy(
            src_ref=outgoing.at[level, piece], dst_ref=incoming.at[level, piece],
            send_sem=s_send.at[level], recv_sem=s_recv.at[level, group],
            device_id=(me ^ (1 << level), core), device_id_type=MESH,
        )

    def sum_needed(level):
        return me // 2 ** (level + 1) != n // 2 ** (level + 1) - 1

    def active(level):
        return me // 2**level % 2 == 1

    def sends(level):
        return jnp.logical_or(jnp.logical_not(active(level)), sum_needed(level))

    def receives(level):
        return jnp.logical_or(active(level), sum_needed(level))

    def first_copy(part, slot, target, half):
        g, lo, size, _ = parts[part]
        return pltpu.make_async_remote_copy(
            src_ref=w_ref.at[0, :, pl.ds(half * cols + lo, size)],
            dst_ref=wbuf.at[g, me, :, pl.ds(lo, size)],
            send_sem=w_send.at[part, slot], recv_sem=w_recv.at[part, me],
            device_id=(target, half), device_id_type=MESH,
        )

    def first(part, ranks):
        g, _, _, order = parts[part]
        for rank in ranks:
            d = order[rank]
            length, stride = dims[d]
            for slot, step in ((2 * rank, 1), (2 * rank + 1, -1)):
                ok = jnp.logical_and(place[d] + step >= 0, place[d] + step < length)

                @pl.when(jnp.logical_and(ok, core == g))
                def _():
                    for half in range(2):
                        first_copy(part, slot, me + step * stride, half).start()

    def weight_copy(part, source, slot, target):
        g, lo, size, _ = parts[part]
        piece = wbuf.at[g, source, :, pl.ds(lo, size)]
        return pltpu.make_async_remote_copy(
            src_ref=piece, dst_ref=piece,
            send_sem=w_send.at[part, slot], recv_sem=w_recv.at[part, source],
            device_id=(target, core), device_id_type=MESH,
        )

    def forward(part, ks):
        order = parts[part][3]
        at = {d: nearest(k, place[d], dims[d][0]) for d, k in zip(order, ks)}
        source = sum(at[d] * dims[d][1] for d in at)
        arrived = max(r for r, k in enumerate(ks) if k)
        weight_copy(part, source, 0, me).wait_recv()
        for rank in range(arrived, len(order)):
            d = order[rank]
            length, stride = dims[d]
            for slot, step in ((2 * rank, 1), (2 * rank + 1, -1)):
                if rank == arrived and length == 2:
                    continue
                ok = jnp.logical_and(place[d] + step >= 0, place[d] + step < length)
                if rank == arrived:
                    ok = jnp.logical_and(ok, (place[d] - at[d]) * step > 0)

                @pl.when(ok)
                def _():
                    weight_copy(part, source, slot, me + step * stride).start()

    def sent(part):
        g, lo, size, order = parts[part]
        ahead = 1
        for rank, d in enumerate(order):
            length = dims[d][0]
            for slot, up in ((2 * rank, True), (2 * rank + 1, False)):
                for p in range(length - 1) if up else range(1, length):
                    count = ahead - 1 + ahead * (p if up else length - 1 - p)
                    for mine in (0, 2):
                        if count + mine == 0:
                            continue

                        @pl.when(jnp.logical_and(place[d] == p, (core == g) == (mine == 2)))
                        def _():
                            piece = wbuf.at[g, pl.ds(0, count + mine), :, pl.ds(lo, size)]
                            pltpu.make_async_remote_copy(
                                src_ref=piece, dst_ref=piece, send_sem=w_send.at[part, slot], recv_sem=w_recv.at[part, 0],
                                device_id=(me, other), device_id_type=MESH,
                            ).wait_send()

            ahead *= length

    def make_mix():
        ids = lax.broadcasted_iota(jnp.int32, (table_ref.shape[0], tokens), 0)
        one_hot = (ids == pattern_ref[...].reshape(1, tokens)).astype(jnp.float32)
        mix = lax.dot_general(
            one_hot, table_ref[...], (((0,), (0,)), ((), ())),
            precision=lax.Precision.HIGHEST, preferred_element_type=jnp.float32,
        )
        for l in range(bits + 1):
            factor = 1.0 / math.sqrt(tokens * (1 if l == 0 else 2 ** (l - 1)))
            mixb[l] = jnp.broadcast_to(mix[:, l : l + 1] * factor, (tokens, HD))

    def state_start(group):
        loaded("k", "v")
        for h in range(group * per, (group + 1) * per):
            state = lax.dot_general(
                k_ref[:, head_cols(h)], v_ref[:, head_cols(h)], (((0,), (0,)), ((), ())),
                preferred_element_type=jnp.float32,
            )
            sub[h] = state
            outgoing[0, h] = state.astype(jnp.bfloat16)

        @pl.when(sends(0))
        def _():
            state_copy(0, group).start()

    def within_event(h):
        columns = head_cols(h)
        scores = lax.dot_general(
            q_ref[:, columns], k_ref[:, columns], (((1,), (1,)), ((), ())),
            preferred_element_type=jnp.float32,
        )
        row = lax.broadcasted_iota(jnp.int32, (tokens, tokens), 0)
        col = lax.broadcasted_iota(jnp.int32, (tokens, tokens), 1)
        inner = jnp.where(col <= row, scores, 0.0).astype(jnp.bfloat16)
        acc[:, columns] = mixb[0] * jnp.dot(inner, v_ref[:, columns], preferred_element_type=jnp.float32)

    def att_copy(group):
        columns = pl.ds(group * per * HD, per * HD)
        return pltpu.make_async_remote_copy(
            src_ref=att.at[core, :, columns], dst_ref=att.at[core, :, columns],
            send_sem=a_send, recv_sem=a_recv,
            device_id=(me, other), device_id_type=MESH,
        )

    def att_whole(which):
        return pltpu.make_async_remote_copy(
            src_ref=att.at[which], dst_ref=att.at[which], send_sem=a_send, recv_sem=a_recv,
            device_id=(me, other), device_id_type=MESH,
        )

    def state_event(level, group):
        @pl.when(receives(level))
        def _():
            state_copy(level, group).wait_recv()

        span = range(group * per, (group + 1) * per)
        if level + 1 < bits:
            @pl.when(sum_needed(level))
            def _():
                for h in span:
                    summed = sub[h] + incoming[level, h].astype(jnp.float32)
                    sub[h] = summed
                    outgoing[level + 1, h] = summed.astype(jnp.bfloat16)

            @pl.when(sends(level + 1))
            def _():
                state_copy(level + 1, group).start()

    def read_event(level, group):
        @pl.when(active(level))
        def _():
            for h in range(group * per, (group + 1) * per):
                acc[:, head_cols(h)] += mixb[level + 1] * jnp.dot(
                    q_ref[:, head_cols(h)], incoming[level, h], preferred_element_type=jnp.float32
                )

        if level + 1 == bits:
            columns = slice(group * per * HD, (group + 1) * per * HD)
            att[core, :, columns] = acc[:, columns].astype(jnp.bfloat16)
            att_copy(group).start()

    def project(part, k):
        g, lo, size, _ = parts[part]
        length, stride = dims[0]
        slab = nearest(k, place[0], length) * stride
        depth = stride * rows
        piece = wbuf[g, pl.ds(slab, stride), :, lo : lo + size].reshape(depth, size)
        taken = att[g, :, pl.ds(pl.multiple_of(slab * rows, math.gcd(depth, 1024)), depth)]
        out_ref[:, lo : lo + size] += jnp.dot(taken, piece, preferred_element_type=jnp.float32)

    for event in events:
        kind, args = event[0], event[1:]
        if kind == "first":
            first(*args)
        elif kind == "pair":
            pair_copy(core).start()
            own.start()
        elif kind == "paired":
            own.wait()
            pair_copy(other).wait_recv()
        elif kind == "start":
            state_start(*args)
        elif kind == "mix":
            make_mix()
            out_ref[...] = jnp.zeros_like(out_ref)
        elif kind == "within":
            loaded("k", "v", "q")
            within_event(*args)
        elif kind == "state":
            state_event(*args)
        elif kind == "read":
            read_event(*args)
        elif kind == "weight":
            forward(*args)
        elif kind == "att":
            att_whole(other).wait_recv()
        elif kind == "project":
            project(*args)

    pair_copy(core).wait_send()
    att_whole(core).wait_send()
    for level in range(bits):
        @pl.when(sends(level))
        def _():
            pltpu.make_async_remote_copy(
                src_ref=outgoing.at[level], dst_ref=incoming.at[level],
                send_sem=s_send.at[level], recv_sem=s_recv.at[level, 0],
                device_id=(me ^ (1 << level), core), device_id_type=MESH,
            ).wait_send()
    for part in range(len(parts)):
        sent(part)


def make_parts(dims, tiles):
    long = max(range(3), key=lambda i: dims[i][0])
    a, b = [i for i in range(3) if i != long]
    direct = max(1, tiles // 8)
    most = (tiles - direct + 1) // 2
    parts = []
    for g, sizes in enumerate(((most, tiles - direct - most, direct), (tiles - direct - most, most, direct))):
        last = (b, a, long) if g == 0 else (a, b, long)
        lo = 0
        for size, order in zip(sizes, ((long, b, a), (long, a, b), last)):
            parts.append((g, lo * 128, size * 128, order))
            lo += size
    return parts


def make_events(dims, parts, n, heads, groups):
    bits = n.bit_length() - 1
    timed = []
    for part, (_, _, _, order) in enumerate(parts):
        for rank, d in enumerate(order):
            timed.append(((0, rank, part), ("first", part, (rank,))))
    for group in range(groups):
        timed.append(((1, group), ("start", group)))
    for h in range(heads):
        timed.append(((3 + h, 9), ("within", h)))
    for level in range(bits):
        for group in range(groups):
            timed.append(((3 + 3 * level + group, 0), ("state", level, group)))
    for part, (_, _, _, order) in enumerate(parts):
        for ks in itertools.product(*[range(dims[d][0]) for d in order]):
            if any(ks):
                timed.append(((3 * sum(1 for k in ks if k) + sum(ks), part), ("weight", part, ks)))
    if ORDER and len(ORDER) == len(timed) and [d[0] for d in dims] == LENGTHS:
        chosen = [timed[i][1] for i in ORDER]
    else:
        chosen = [event for _, event in sorted(timed, key=lambda t: t[0])]
    events, inside = [], []
    for event in chosen:
        if event[0] == "within" and event[1] in inside:
            continue
        due = [event[1]] if event[0] == "within" else []
        if event[0] == "state":
            events.append(event)
            per = heads // groups
            due = [h for h in range(event[2] * per, (event[2] + 1) * per) if h not in inside]
        if due and not inside:
            events.append(("mix",))
        events += [("within", h) for h in due]
        inside += due
        if event[0] == "state":
            events.append(("read",) + event[1:])
        elif event[0] != "within":
            events.append(event)
    at = 1 + max(i for i, e in enumerate(events) if e[0] == "start")
    events.insert(at, ("pair",))
    reads = max(i for i, e in enumerate(events) if e[0] == "read")
    at = min(len(events), reads + 1 + LAG)
    events[at:at] = [("paired",), ("att",)]
    ready = {}
    for i, e in enumerate(events):
        if e[0] == "weight":
            key = (e[1], e[2][parts[e[1]][3].index(0)])
            ready[key] = max(ready.get(key, at + 1), i)
    placed, queue = [], []
    for i, e in enumerate(events):
        placed.append(e)
        queue += sorted((key for key, j in ready.items() if j == i), key=lambda key: key[::-1])
        if queue and i + 1 < len(events):
            placed.append(("project",) + queue.pop(0))
    placed += [("project",) + key for key in queue]
    return placed


def planned(dims, queries, keys, values, level_pattern, level_weight, out_weight):
    n = lax.axis_size("seq")
    tokens, width = queries.shape
    heads = width // HD
    bits = n.bit_length() - 1
    _, rows, full = out_weight.shape
    cols = full // 2
    groups = min(4, heads)
    parts = make_parts(dims, cols // 128)
    events = make_events(dims, parts, n, heads, groups)
    bf16, f32 = jnp.bfloat16, jnp.float32
    any_spec = pl.BlockSpec(memory_space=pl.ANY)
    vmem_spec = pl.BlockSpec(memory_space=pltpu.VMEM)
    dma = pltpu.SemaphoreType.DMA
    return pl.pallas_call(
        functools.partial(planned_kernel, (dims, parts, events, n)),
        out_shape=pltpu.VMEM((tokens, cols), f32),
        in_specs=[any_spec] * 3 + [vmem_spec] * 2 + [any_spec],
        out_specs=vmem_spec,
        scratch_shapes=[
            pltpu.VMEM((tokens, width), bf16),
            pltpu.VMEM((tokens, width), bf16),
            pltpu.VMEM((tokens, width), bf16),
            pltpu.VMEM((1, rows, full), bf16),
            pltpu.VMEM((2, n, rows, cols), bf16),
            pltpu.VMEM((2, tokens, width), bf16),
            pltpu.VMEM((tokens, width), f32),
            pltpu.VMEM((heads, HD, HD), f32),
            pltpu.VMEM((bits, heads, HD, HD), bf16),
            pltpu.VMEM((bits, heads, HD, HD), bf16),
            pltpu.VMEM((bits + 1, tokens, HD), f32),
            dma((4,)),
            dma,
            dma,
            dma,
            dma((len(parts), 2 * len(dims))),
            dma((len(parts), n)),
            dma((bits,)),
            dma((bits, groups)),
            dma,
            dma,
        ],
        compiler_params=pltpu.CompilerParams(
            collective_id=0, has_side_effects=True, vmem_limit_bytes=60 * 2**20
        ),
    )(queries, keys, values, level_pattern, level_weight, out_weight)


def on_device(dims, queries, keys, values, level_pattern, level_weight, out_weight):
    n = lax.axis_size("seq")
    tokens, width = queries.shape
    heads = width // HD
    bits = n.bit_length() - 1
    _, rows, full = out_weight.shape
    cols = full // 2
    fused = rows % 16 == 0
    if fused and len(dims) == 3 and cols % 1024 == 0:
        return planned(dims, queries, keys, values, level_pattern, level_weight, out_weight)
    groups = min(4, heads)
    tiles = cols // 128
    if len(dims) == 3:
        long = max(range(3), key=lambda i: dims[i][0])
        a, b = [i for i in range(3) if i != long]
        orders = [(long, a, b), (long, b, a), (a, b, long)]
        share = max(1, tiles * 3 // 8)
        sizes = [share, share, tiles - 2 * share]
    else:
        orders, sizes = [tuple(range(len(dims)))], [tiles]
    cuts, lo = [], 0
    for size in sizes:
        cuts.append((lo * 128, size * 128))
        lo += size
    events = schedule(dims, orders, cuts, n, heads, groups, fused)
    plan = (dims, orders, cuts, events, n, fused)
    bf16, f32 = jnp.bfloat16, jnp.float32
    any_spec = pl.BlockSpec(memory_space=pl.ANY)
    vmem_spec = pl.BlockSpec(memory_space=pltpu.VMEM)
    if fused:
        out_shape = pltpu.VMEM((tokens, cols), f32)
        out_specs = vmem_spec
    else:
        out_shape = [
            jax.ShapeDtypeStruct((2, tokens, width), bf16),
            jax.ShapeDtypeStruct((2, n, rows, cols), bf16),
        ]
        out_specs = [any_spec, any_spec]
    dma = pltpu.SemaphoreType.DMA
    result = pl.pallas_call(
        functools.partial(kernel, plan),
        out_shape=out_shape,
        in_specs=[any_spec] * 3 + [vmem_spec] * 2 + [any_spec],
        out_specs=out_specs,
        scratch_shapes=[
            pltpu.VMEM((tokens, width), bf16),
            pltpu.VMEM((tokens, width), bf16),
            pltpu.VMEM((tokens, width), bf16),
            pltpu.VMEM((1, rows, full), bf16),
            pltpu.VMEM((2, n, rows, cols), bf16),
            pltpu.VMEM((2, tokens, width), bf16),
            pltpu.VMEM((tokens, width), f32),
            pltpu.VMEM((heads, HD, HD), f32),
            pltpu.VMEM((bits, heads, HD, HD), bf16),
            pltpu.VMEM((bits, heads, HD, HD), bf16),
            pltpu.VMEM((bits + 1, tokens, HD), f32),
            dma((4,)),
            dma,
            dma,
            dma,
            dma((len(orders), n if fused else 1, 2 * len(dims))),
            dma((len(orders), n)),
            dma((bits, groups)),
            dma((bits, groups)),
            dma((groups,)),
            dma((groups,)),
        ],
        compiler_params=pltpu.CompilerParams(
            collective_id=0, has_side_effects=True, vmem_limit_bytes=60 * 2**20
        ),
    )(queries, keys, values, level_pattern, level_weight, out_weight)
    if fused:
        return result
    att, gathered = result
    return jnp.einsum(
        "gtk,gkd->td", att, gathered.reshape(2, n * rows, cols), preferred_element_type=f32
    )


def solution(mesh):
    placed = (
        P("seq", "head"),
        P("seq", "head"),
        P("seq", "head"),
        P("seq"),
        P(),
        P("head", "seq", None),
    )
    return jax.shard_map(
        functools.partial(on_device, line_dims(mesh)),
        mesh=mesh, in_specs=placed, out_specs=P("seq", "head"), check_vma=False,
    )
```

```python
import functools
import itertools
import math

import jax
import jax.numpy as jnp
from jax import lax
from jax.experimental import pallas as pl
from jax.experimental.pallas import tpu as pltpu
from jax.sharding import PartitionSpec as P

HD = 128
MESH = pl.DeviceIdType.MESH
ORDER = (15, 0, 4, 16, 9, 10, 13, 18, 19, 22, 3, 20, 6, 8, 12, 7, 21, 17, 11, 30, 2, 14, 64, 31, 94, 53, 29, 5, 32, 49, 1, 92, 79, 113, 122, 109, 121, 68, 34, 25, 123, 128, 33, 46, 98, 35, 61, 66, 107, 80, 62, 36, 95, 83, 77, 124, 38, 24, 47, 28, 57, 76, 40, 106, 51, 93, 65, 39, 26, 117, 72, 102, 111, 81, 129, 37, 132, 27, 44, 108, 42, 100, 87, 130, 125, 55, 23, 59, 84, 41, 115, 91, 43, 73, 69, 103, 45, 88, 70, 96, 134, 52, 114, 133, 131, 58, 82, 54, 104, 74, 101, 99, 89, 63, 135, 50, 90, 110, 119, 86, 85, 126, 56, 71, 67, 118, 127, 60, 48, 75, 97, 78, 116, 112, 120, 105,)
LENGTHS = [4, 2, 2]
LAG = 6


def line_dims(mesh):
    n = mesh.shape["seq"]
    devices = mesh.devices.reshape(n, -1)[:, 0]
    coords = [tuple(getattr(d, "coords", ())) for d in devices]
    dims = []
    if len(set(coords)) == n:
        for axis in range(len(coords[0])):
            seen = [c[axis] - coords[0][axis] for c in coords]
            length = max(seen) + 1
            if length > 1:
                dims.append((length, seen.index(1)))
    stride = 1
    for length, step in sorted(dims, key=lambda d: d[1]):
        if step != stride:
            break
        stride *= length
    if not dims or stride != n:
        dims = [(2, 1 << i) for i in range(n.bit_length() - 1)]
    return sorted(dims, key=lambda d: -d[1])


def nearest(k, p, n):
    m = jnp.minimum(p, n - 1 - p)
    sign = jnp.where(p == m, 1, -1)
    near = (k + 1) // 2 * (2 * (k % 2) - 1)
    if n == 2:
        return p + k * (1 - 2 * p)
    return jnp.where(k <= 2 * m, p + near, p + sign * (k - m))


def kernel(
    plan, q_hbm, k_hbm, v_hbm, pattern_ref, table_ref, w_hbm, *rest
):
    dims, orders, cuts, events, n, fused = plan
    if fused:
        out_ref, *rest = rest
    else:
        att_hbm, w_out_hbm, *rest = rest
    (q_ref, k_ref, v_ref, w_ref, wbuf, att, acc, sub, outgoing, incoming, mixb,
     load_sem, own_sem, pair_send, pair_recv, w_send, w_recv, s_send, s_recv, a_send, a_recv) = rest
    me = lax.axis_index("seq")
    core = lax.axis_index("head")
    other = 1 - core
    tokens, width = q_ref.shape
    heads = width // HD
    cols = wbuf.shape[-1]
    bits = n.bit_length() - 1
    groups = a_send.shape[0]
    per = heads // groups
    place = [me // stride % length for length, stride in dims]

    loads = [
        pltpu.make_async_copy(src, dst, load_sem.at[i])
        for i, (src, dst) in enumerate(((w_hbm, w_ref), (k_hbm, k_ref), (v_hbm, v_ref), (q_hbm, q_ref)))
    ]
    for load in loads:
        load.start()

    barrier = pltpu.get_barrier_semaphore()
    total = 1
    pl.semaphore_signal(barrier, inc=1, device_id=(me, other), device_id_type=MESH)
    for bit in range(bits):
        pl.semaphore_signal(barrier, inc=1, device_id=(me ^ (1 << bit), core), device_id_type=MESH)
        total += 1
    for (length, stride), p in zip(dims, place):
        if length == 2:
            continue
        for step in (-1, 1):
            there = jnp.logical_and(p + step >= 0, p + step < length)

            @pl.when(there)
            def _():
                pl.semaphore_signal(barrier, inc=1, device_id=(me + step * stride, core), device_id_type=MESH)

            total = total + there.astype(jnp.int32)

    for l in range(bits + 1):
        if l == 0:
            ids = lax.broadcasted_iota(jnp.int32, (table_ref.shape[0], tokens), 0)
            one_hot = (ids == pattern_ref[...].reshape(1, tokens)).astype(jnp.float32)
            mix = lax.dot_general(
                one_hot, table_ref[...], (((0,), (0,)), ((), ())),
                precision=lax.Precision.HIGHEST, preferred_element_type=jnp.float32,
            )
        factor = 1.0 / math.sqrt(tokens * (1 if l == 0 else 2 ** (l - 1)))
        mixb[l] = jnp.broadcast_to(mix[:, l : l + 1] * factor, (tokens, HD))

    def head_cols(h):
        return slice(h * HD, (h + 1) * HD)

    loads[1].wait()
    loads[2].wait()

    def make_states(h):
        state = lax.dot_general(
            k_ref[:, head_cols(h)], v_ref[:, head_cols(h)], (((0,), (0,)), ((), ())),
            preferred_element_type=jnp.float32,
        )
        sub[h] = state
        outgoing[0, h] = state.astype(jnp.bfloat16)

    for h in range(heads):
        make_states(h)
    loads[0].wait()
    pl.semaphore_wait(barrier, total)

    def pair_copy():
        return pltpu.make_async_remote_copy(
            src_ref=w_ref.at[0, :, pl.ds(pl.multiple_of(other * cols, 128), cols)],
            dst_ref=wbuf.at[core, me], send_sem=pair_send, recv_sem=pair_recv,
            device_id=(me, other), device_id_type=MESH,
        )

    def pair_landed():
        return pltpu.make_async_remote_copy(
            src_ref=w_ref.at[0, :, pl.ds(pl.multiple_of(other * cols, 128), cols)],
            dst_ref=wbuf.at[other, me], send_sem=pair_send, recv_sem=pair_recv,
            device_id=(me, other), device_id_type=MESH,
        )

    pair_copy().start()
    own = pltpu.make_async_copy(
        w_ref.at[0, :, pl.ds(pl.multiple_of(core * cols, 128), cols)], wbuf.at[core, me], own_sem
    )
    own.start()

    def state_copy(level, group):
        piece = pl.ds(group * per, per)
        return pltpu.make_async_remote_copy(
            src_ref=outgoing.at[level, piece], dst_ref=incoming.at[level, piece],
            send_sem=s_send.at[level, group], recv_sem=s_recv.at[level, group],
            device_id=(me ^ (1 << level), core), device_id_type=MESH,
        )

    def sum_needed(level):
        return me // 2 ** (level + 1) != n // 2 ** (level + 1) - 1

    def active(level):
        return me // 2**level % 2 == 1

    def sends(level):
        return jnp.logical_or(jnp.logical_not(active(level)), sum_needed(level))

    def receives(level):
        return jnp.logical_or(active(level), sum_needed(level))

    for group in range(groups):
        @pl.when(sends(0))
        def _():
            state_copy(0, group).start()

    def weight_copy(part, source, slot, target):
        lo, size = cuts[part]
        piece = wbuf.at[:, source, :, pl.ds(lo, size)]
        return pltpu.make_async_remote_copy(
            src_ref=piece, dst_ref=piece,
            send_sem=w_send.at[part, source if fused else 0, slot], recv_sem=w_recv.at[part, source],
            device_id=(target, core), device_id_type=MESH,
        )

    def forward(part, source, at, arrived, action):
        order = orders[part]
        for rank in range(max(arrived, 0), len(order)):
            d = order[rank]
            length, stride = dims[d]
            for slot, step in ((2 * rank, 1), (2 * rank + 1, -1)):
                if rank == arrived and length == 2:
                    continue
                ok = jnp.logical_and(place[d] + step >= 0, place[d] + step < length)
                if rank == arrived:
                    ok = jnp.logical_and(ok, (place[d] - at[d]) * step > 0)

                @pl.when(ok)
                def _():
                    copy = weight_copy(part, source, slot, me + step * stride)
                    if action == "start":
                        copy.start()
                    else:
                        copy.wait_send()

    def source_of(part, ks):
        at = {d: nearest(k, place[d], dims[d][0]) for d, k in zip(orders[part], ks)}
        return at, sum(at[d] * dims[d][1] for d in at)

    def arrived_by(ks):
        return max((r for r, k in enumerate(ks) if k), default=-1)

    def weight_event(part, ks, arrived):
        at, source = source_of(part, ks)
        weight_copy(part, source, 0, me).wait_recv()
        forward(part, source, at, arrived, "start")
        if not fused:
            forward(part, source, at, arrived, "wait")

    def read_state(level, h):
        acc[:, head_cols(h)] += mixb[level + 1] * jnp.dot(
            q_ref[:, head_cols(h)], incoming[level, h], preferred_element_type=jnp.float32
        )

    def within_event(h):
        columns = head_cols(h)
        scores = lax.dot_general(
            q_ref[:, columns], k_ref[:, columns], (((1,), (1,)), ((), ())),
            preferred_element_type=jnp.float32,
        )
        row = lax.broadcasted_iota(jnp.int32, (tokens, tokens), 0)
        col = lax.broadcasted_iota(jnp.int32, (tokens, tokens), 1)
        inner = jnp.where(col <= row, scores, 0.0).astype(jnp.bfloat16)
        acc[:, columns] = mixb[0] * jnp.dot(inner, v_ref[:, columns], preferred_element_type=jnp.float32)

    def att_copy(group, mine):
        columns = pl.ds(group * per * HD, per * HD)
        which = core if mine else other
        return pltpu.make_async_remote_copy(
            src_ref=att.at[core, :, columns], dst_ref=att.at[which, :, columns],
            send_sem=a_send.at[group], recv_sem=a_recv.at[group],
            device_id=(me, other), device_id_type=MESH,
        )

    def state_event(level, group):
        @pl.when(receives(level))
        def _():
            state_copy(level, group).wait_recv()

        span = range(group * per, (group + 1) * per)
        if level + 1 < bits:
            @pl.when(sum_needed(level))
            def _():
                for h in span:
                    summed = sub[h] + incoming[level, h].astype(jnp.float32)
                    sub[h] = summed
                    outgoing[level + 1, h] = summed.astype(jnp.bfloat16)

            @pl.when(sends(level + 1))
            def _():
                state_copy(level + 1, group).start()

        @pl.when(active(level))
        def _():
            for h in span:
                read_state(level, h)

        if level + 1 == bits:
            columns = slice(group * per * HD, (group + 1) * per * HD)
            att[core, :, columns] = acc[:, columns].astype(jnp.bfloat16)
            att_copy(group, True).start()

    own.wait()
    pair_landed().wait_recv()
    for part in range(len(orders)):
        at, source = source_of(part, (0,) * len(dims))
        forward(part, source, at, -1, "start")
        if not fused:
            forward(part, source, at, -1, "wait")
    loads[3].wait()

    def project(part):
        lo, size = cuts[part]
        columns = slice(lo, lo + size)
        flat = [wbuf[g, :, :, columns].reshape(-1, size) for g in range(2)]
        out_ref[:, columns] = jnp.dot(att[0], flat[0], preferred_element_type=jnp.float32) + jnp.dot(
            att[1], flat[1], preferred_element_type=jnp.float32
        )

    for event in events:
        if event[0] == "within":
            within_event(event[1])
        elif event[0] == "state":
            state_event(event[1], event[2])
        elif event[0] == "weight":
            weight_event(*event[1:])
        elif event[0] == "loop":
            lengths = [[dims[d][0] for d in order] for order in orders]

            def each(e, carry):
                for part, order in enumerate(orders):
                    for arrived in range(len(order)):
                        below = math.prod(lengths[part][:arrived])
                        ks = []
                        rest_e = e
                        for length in lengths[part]:
                            ks.append(rest_e % length)
                            rest_e = rest_e // length

                        @pl.when(jnp.logical_and(e >= below, e < below * lengths[part][arrived]))
                        def _():
                            weight_event(part, ks, arrived)

                return carry

            lax.fori_loop(1, n, each, 0)
        elif event[0] == "att":
            for group in range(groups):
                att_copy(group, False).wait_recv()
        elif event[0] == "project" and fused:
            project(event[1])

    def finish(part, e):
        ks = []
        for d in orders[part]:
            ks.append(e % dims[d][0])
            e = e // dims[d][0]
        return ks

    pair_copy().wait_send()
    for group in range(groups):
        att_copy(group, True).wait_send()
        for level in range(bits):
            @pl.when(sends(level))
            def _():
                state_copy(level, group).wait_send()
    if fused:
        for part in range(len(orders)):
            for e in range(n):
                ks = finish(part, e)
                at, source = source_of(part, ks)
                forward(part, source, at, arrived_by(ks), "wait")
    if not fused:
        stores = [pltpu.make_async_copy(att, att_hbm, load_sem.at[0]), pltpu.make_async_copy(wbuf, w_out_hbm, load_sem.at[1])]
        for store in stores:
            store.start()
        for store in stores:
            store.wait()


def schedule(dims, orders, cuts, n, heads, groups, unrolled):
    bits = n.bit_length() - 1
    whole = sum(size for _, size in cuts)
    timed = []
    for h in range(heads):
        timed.append((0.35 * h / heads, ("within", h)))
    for level in range(bits):
        for group in range(groups):
            timed.append((0.45 + 0.75 * level + 0.25 * group, ("state", level, group)))
    if not unrolled:
        tail = [("loop",), ("att",)]
    else:
        last = {}
        for part, order in enumerate(orders):
            lengths = [dims[d][0] for d in order]
            count = [0] * len(order)
            for rev in itertools.product(*[range(length) for length in lengths[::-1]]):
                ks = rev[::-1]
                arrived = max((r for r, k in enumerate(ks) if k), default=-1)
                if arrived < 0:
                    continue
                count[arrived] += 1
                when = count[arrived] * cuts[part][1] / whole * 1.8 + 0.3 * sum(1 for k in ks if k)
                if arrived == len(order) - 1 and lengths[-1] == 2:
                    when += 100
                timed.append((when, ("weight", part, ks, arrived)))
        tail = [("att",)]
    timed.sort(key=lambda t: t[0])
    return [e for _, e in timed] + tail + [("project", p) for p in range(len(orders))]


def planned_kernel(
    plan, q_hbm, k_hbm, v_hbm, pattern_ref, table_ref, w_hbm, out_ref,
    q_ref, k_ref, v_ref, w_ref, wbuf, att, acc, sub, outgoing, incoming, mixb,
    load_sem, own_sem, pair_send, pair_recv, w_send, w_recv, s_send, s_recv, a_send, a_recv,
):
    dims, parts, events, n = plan
    me = lax.axis_index("seq")
    core = lax.axis_index("head")
    other = 1 - core
    tokens, width = q_ref.shape
    rows = w_ref.shape[1]
    heads = width // HD
    cols = wbuf.shape[-1]
    bits = n.bit_length() - 1
    groups = s_recv.shape[1]
    per = heads // groups
    place = [me // stride % length for length, stride in dims]

    loads = {
        name: pltpu.make_async_copy(src, dst, load_sem.at[i])
        for i, (name, src, dst) in enumerate(
            (("w", w_hbm, w_ref), ("k", k_hbm, k_ref), ("v", v_hbm, v_ref), ("q", q_hbm, q_ref))
        )
    }
    for load in loads.values():
        load.start()

    barrier = pltpu.get_barrier_semaphore()
    total = 1
    pl.semaphore_signal(barrier, inc=1, device_id=(me, other), device_id_type=MESH)
    for (length, stride), p in zip(dims, place):
        for step in (-1, 1):
            there = jnp.logical_and(p + step >= 0, p + step < length)

            @pl.when(there)
            def _():
                for c in range(2):
                    pl.semaphore_signal(barrier, inc=1, device_id=(me + step * stride, c), device_id_type=MESH)

            total = total + 2 * there.astype(jnp.int32)
    for bit in range(bits - 1):
        if all(1 << bit != stride for _, stride in dims):
            pl.semaphore_signal(barrier, inc=1, device_id=(me ^ (1 << bit), core), device_id_type=MESH)
            total = total + 1

    waited = set()

    def loaded(*names):
        for name in names:
            if name not in waited:
                waited.add(name)
                loads[name].wait()

    loaded("w")
    pl.semaphore_wait(barrier, total)

    def head_cols(h):
        return slice(h * HD, (h + 1) * HD)

    def pair_copy(which):
        return pltpu.make_async_remote_copy(
            src_ref=w_ref.at[0, :, pl.ds(pl.multiple_of(other * cols, 128), cols)],
            dst_ref=wbuf.at[which, me], send_sem=pair_send, recv_sem=pair_recv,
            device_id=(me, other), device_id_type=MESH,
        )

    own = pltpu.make_async_copy(
        w_ref.at[0, :, pl.ds(pl.multiple_of(core * cols, 128), cols)], wbuf.at[core, me], own_sem
    )

    top = bits - 1
    reach, climb = dims[0]

    def state_copy(level, group, relay=False):
        piece = pl.ds(group * per, per)
        target = me + climb if level == top else me ^ (1 << level)
        return pltpu.make_async_remote_copy(
            src_ref=(incoming if relay else outgoing).at[level, piece], dst_ref=incoming.at[level, piece],
            send_sem=s_send.at[level], recv_sem=s_recv.at[level, group],
            device_id=(target, core), device_id_type=MESH,
        )

    def sum_needed(level, who=me):
        if level == top - 1:
            return who // climb == reach // 2 - 1
        return who // 2 ** (level + 1) != n // 2 ** (level + 1) - 1

    def active(level, who=me):
        return who // 2**level % 2 == 1

    def receives(level, who=me):
        if level == top:
            return active(level, who)
        return jnp.logical_or(active(level, who), sum_needed(level, who))

    def sends(level):
        if level == top:
            return place[0] == reach // 2 - 1
        return receives(level, me ^ (1 << level))

    relays = jnp.logical_and(active(top), place[0] < reach - 1)

    def first_copy(part, slot, target, half):
        g, lo, size, _ = parts[part]
        return pltpu.make_async_remote_copy(
            src_ref=w_ref.at[0, :, pl.ds(half * cols + lo, size)],
            dst_ref=wbuf.at[g, me, :, pl.ds(lo, size)],
            send_sem=w_send.at[part, slot], recv_sem=w_recv.at[part, me],
            device_id=(target, half), device_id_type=MESH,
        )

    def first(part, ranks):
        g, _, _, order = parts[part]
        for rank in ranks:
            d = order[rank]
            length, stride = dims[d]
            for slot, step in ((2 * rank, 1), (2 * rank + 1, -1)):
                ok = jnp.logical_and(place[d] + step >= 0, place[d] + step < length)

                @pl.when(jnp.logical_and(ok, core == g))
                def _():
                    for half in range(2):
                        first_copy(part, slot, me + step * stride, half).start()

    def weight_copy(part, source, slot, target):
        g, lo, size, _ = parts[part]
        piece = wbuf.at[g, source, :, pl.ds(lo, size)]
        return pltpu.make_async_remote_copy(
            src_ref=piece, dst_ref=piece,
            send_sem=w_send.at[part, slot], recv_sem=w_recv.at[part, source],
            device_id=(target, core), device_id_type=MESH,
        )

    def forward(part, ks):
        order = parts[part][3]
        at = {d: nearest(k, place[d], dims[d][0]) for d, k in zip(order, ks)}
        source = sum(at[d] * dims[d][1] for d in at)
        arrived = max(r for r, k in enumerate(ks) if k)
        weight_copy(part, source, 0, me).wait_recv()
        for rank in range(arrived, len(order)):
            d = order[rank]
            length, stride = dims[d]
            for slot, step in ((2 * rank, 1), (2 * rank + 1, -1)):
                if rank == arrived and length == 2:
                    continue
                ok = jnp.logical_and(place[d] + step >= 0, place[d] + step < length)
                if rank == arrived:
                    ok = jnp.logical_and(ok, (place[d] - at[d]) * step > 0)

                @pl.when(ok)
                def _():
                    weight_copy(part, source, slot, me + step * stride).start()

    def sent(part):
        g, lo, size, order = parts[part]
        ahead = 1
        for rank, d in enumerate(order):
            length = dims[d][0]
            for slot, up in ((2 * rank, True), (2 * rank + 1, False)):
                for p in range(length - 1) if up else range(1, length):
                    count = ahead - 1 + ahead * (p if up else length - 1 - p)
                    for mine in (0, 2):
                        if count + mine == 0:
                            continue

                        @pl.when(jnp.logical_and(place[d] == p, (core == g) == (mine == 2)))
                        def _():
                            piece = wbuf.at[g, pl.ds(0, count + mine), :, pl.ds(lo, size)]
                            pltpu.make_async_remote_copy(
                                src_ref=piece, dst_ref=piece, send_sem=w_send.at[part, slot], recv_sem=w_recv.at[part, 0],
                                device_id=(me, other), device_id_type=MESH,
                            ).wait_send()

            ahead *= length

    def make_mix():
        ids = lax.broadcasted_iota(jnp.int32, (table_ref.shape[0], tokens), 0)
        one_hot = (ids == pattern_ref[...].reshape(1, tokens)).astype(jnp.float32)
        mix = lax.dot_general(
            one_hot, table_ref[...], (((0,), (0,)), ((), ())),
            precision=lax.Precision.HIGHEST, preferred_element_type=jnp.float32,
        )
        for l in range(bits + 1):
            factor = 1.0 / math.sqrt(tokens * (1 if l == 0 else 2 ** (l - 1)))
            mixb[l] = jnp.broadcast_to(mix[:, l : l + 1] * factor, (tokens, HD))

    def state_start(group):
        loaded("k", "v")
        for h in range(group * per, (group + 1) * per):
            state = lax.dot_general(
                k_ref[:, head_cols(h)], v_ref[:, head_cols(h)], (((0,), (0,)), ((), ())),
                preferred_element_type=jnp.float32,
            )
            sub[h] = state
            outgoing[0, h] = state.astype(jnp.bfloat16)

        @pl.when(sends(0))
        def _():
            state_copy(0, group).start()

    def within_event(h):
        columns = head_cols(h)
        scores = lax.dot_general(
            q_ref[:, columns], k_ref[:, columns], (((1,), (1,)), ((), ())),
            preferred_element_type=jnp.float32,
        )
        row = lax.broadcasted_iota(jnp.int32, (tokens, tokens), 0)
        col = lax.broadcasted_iota(jnp.int32, (tokens, tokens), 1)
        inner = jnp.where(col <= row, scores, 0.0).astype(jnp.bfloat16)
        acc[:, columns] = mixb[0] * jnp.dot(inner, v_ref[:, columns], preferred_element_type=jnp.float32)

    def att_copy(group):
        columns = pl.ds(group * per * HD, per * HD)
        return pltpu.make_async_remote_copy(
            src_ref=att.at[core, :, columns], dst_ref=att.at[core, :, columns],
            send_sem=a_send, recv_sem=a_recv,
            device_id=(me, other), device_id_type=MESH,
        )

    def att_whole(which):
        return pltpu.make_async_remote_copy(
            src_ref=att.at[which], dst_ref=att.at[which], send_sem=a_send, recv_sem=a_recv,
            device_id=(me, other), device_id_type=MESH,
        )

    def state_event(level, group):
        @pl.when(receives(level))
        def _():
            state_copy(level, group).wait_recv()

        span = range(group * per, (group + 1) * per)
        if level + 1 < bits:
            @pl.when(sum_needed(level))
            def _():
                for h in span:
                    summed = sub[h] + incoming[level, h].astype(jnp.float32)
                    sub[h] = summed
                    outgoing[level + 1, h] = summed.astype(jnp.bfloat16)

            @pl.when(sends(level + 1))
            def _():
                state_copy(level + 1, group).start()
        else:
            @pl.when(relays)
            def _():
                state_copy(level, group, True).start()

    def read_event(level, group):
        @pl.when(active(level))
        def _():
            for h in range(group * per, (group + 1) * per):
                acc[:, head_cols(h)] += mixb[level + 1] * jnp.dot(
                    q_ref[:, head_cols(h)], incoming[level, h], preferred_element_type=jnp.float32
                )

        if level + 1 == bits:
            columns = slice(group * per * HD, (group + 1) * per * HD)
            att[core, :, columns] = acc[:, columns].astype(jnp.bfloat16)
            att_copy(group).start()

    def project(part, k):
        g, lo, size, _ = parts[part]
        length, stride = dims[0]
        slab = nearest(k, place[0], length) * stride
        depth = stride * rows
        piece = wbuf[g, pl.ds(slab, stride), :, lo : lo + size].reshape(depth, size)
        taken = att[g, :, pl.ds(pl.multiple_of(slab * rows, math.gcd(depth, 1024)), depth)]
        out_ref[:, lo : lo + size] += jnp.dot(taken, piece, preferred_element_type=jnp.float32)

    for event in events:
        kind, args = event[0], event[1:]
        if kind == "first":
            first(*args)
        elif kind == "pair":
            pair_copy(core).start()
            own.start()
        elif kind == "paired":
            own.wait()
            pair_copy(other).wait_recv()
        elif kind == "start":
            state_start(*args)
        elif kind == "mix":
            make_mix()
            out_ref[...] = jnp.zeros_like(out_ref)
        elif kind == "within":
            loaded("k", "v", "q")
            within_event(*args)
        elif kind == "state":
            state_event(*args)
        elif kind == "read":
            read_event(*args)
        elif kind == "weight":
            forward(*args)
        elif kind == "att":
            att_whole(other).wait_recv()
        elif kind == "project":
            project(*args)

    pair_copy(core).wait_send()
    att_whole(core).wait_send()
    for level in range(bits):
        @pl.when(jnp.logical_or(sends(level), relays) if level == top else sends(level))
        def _():
            pltpu.make_async_remote_copy(
                src_ref=outgoing.at[level], dst_ref=incoming.at[level],
                send_sem=s_send.at[level], recv_sem=s_recv.at[level, 0],
                device_id=(me ^ (1 << level), core), device_id_type=MESH,
            ).wait_send()
    for part in range(len(parts)):
        sent(part)


def make_parts(dims, tiles):
    long = max(range(3), key=lambda i: dims[i][0])
    a, b = [i for i in range(3) if i != long]
    direct = max(1, tiles // 8)
    most = (tiles - direct + 1) // 2
    parts = []
    for g, sizes in enumerate(((most, tiles - direct - most, direct), (tiles - direct - most, most, direct))):
        last = (b, a, long) if g == 0 else (a, b, long)
        lo = 0
        for size, order in zip(sizes, ((long, b, a), (long, a, b), last)):
            parts.append((g, lo * 128, size * 128, order))
            lo += size
    return parts


def make_events(dims, parts, n, heads, groups):
    bits = n.bit_length() - 1
    timed = []
    for part, (_, _, _, order) in enumerate(parts):
        for rank, d in enumerate(order):
            timed.append(((0, rank, part), ("first", part, (rank,))))
    for group in range(groups):
        timed.append(((1, group), ("start", group)))
    for h in range(heads):
        timed.append(((3 + h, 9), ("within", h)))
    for level in range(bits):
        for group in range(groups):
            timed.append(((3 + 3 * level + group, 0), ("state", level, group)))
    for part, (_, _, _, order) in enumerate(parts):
        for ks in itertools.product(*[range(dims[d][0]) for d in order]):
            if any(ks):
                timed.append(((3 * sum(1 for k in ks if k) + sum(ks), part), ("weight", part, ks)))
    if ORDER and len(ORDER) == len(timed) and [d[0] for d in dims] == LENGTHS:
        chosen = [timed[i][1] for i in ORDER]
    else:
        chosen = [event for _, event in sorted(timed, key=lambda t: t[0])]
    events, inside = [], []
    for event in chosen:
        if event[0] == "within" and event[1] in inside:
            continue
        due = [event[1]] if event[0] == "within" else []
        if event[0] == "state":
            events.append(event)
            per = heads // groups
            due = [h for h in range(event[2] * per, (event[2] + 1) * per) if h not in inside]
        if due and not inside:
            events.append(("mix",))
        events += [("within", h) for h in due]
        inside += due
        if event[0] == "state":
            events.append(("read",) + event[1:])
        elif event[0] != "within":
            events.append(event)
    at = 1 + max(i for i, e in enumerate(events) if e[0] == "start")
    events.insert(at, ("pair",))
    reads = max(i for i, e in enumerate(events) if e[0] == "read")
    at = min(len(events), reads + 1 + LAG)
    events[at:at] = [("paired",), ("att",)]
    ready = {}
    for i, e in enumerate(events):
        if e[0] == "weight":
            key = (e[1], e[2][parts[e[1]][3].index(0)])
            ready[key] = max(ready.get(key, at + 1), i)
    placed, queue = [], []
    for i, e in enumerate(events):
        placed.append(e)
        queue += sorted((key for key, j in ready.items() if j == i), key=lambda key: key[::-1])
        if queue and i + 1 < len(events):
            placed.append(("project",) + queue.pop(0))
    placed += [("project",) + key for key in queue]
    return placed


def planned(dims, queries, keys, values, level_pattern, level_weight, out_weight):
    n = lax.axis_size("seq")
    tokens, width = queries.shape
    heads = width // HD
    bits = n.bit_length() - 1
    _, rows, full = out_weight.shape
    cols = full // 2
    groups = min(4, heads)
    parts = make_parts(dims, cols // 128)
    events = make_events(dims, parts, n, heads, groups)
    bf16, f32 = jnp.bfloat16, jnp.float32
    any_spec = pl.BlockSpec(memory_space=pl.ANY)
    vmem_spec = pl.BlockSpec(memory_space=pltpu.VMEM)
    dma = pltpu.SemaphoreType.DMA
    return pl.pallas_call(
        functools.partial(planned_kernel, (dims, parts, events, n)),
        out_shape=pltpu.VMEM((tokens, cols), f32),
        in_specs=[any_spec] * 3 + [vmem_spec] * 2 + [any_spec],
        out_specs=vmem_spec,
        scratch_shapes=[
            pltpu.VMEM((tokens, width), bf16),
            pltpu.VMEM((tokens, width), bf16),
            pltpu.VMEM((tokens, width), bf16),
            pltpu.VMEM((1, rows, full), bf16),
            pltpu.VMEM((2, n, rows, cols), bf16),
            pltpu.VMEM((2, tokens, width), bf16),
            pltpu.VMEM((tokens, width), f32),
            pltpu.VMEM((heads, HD, HD), f32),
            pltpu.VMEM((bits, heads, HD, HD), bf16),
            pltpu.VMEM((bits, heads, HD, HD), bf16),
            pltpu.VMEM((bits + 1, tokens, HD), f32),
            dma((4,)),
            dma,
            dma,
            dma,
            dma((len(parts), 2 * len(dims))),
            dma((len(parts), n)),
            dma((bits,)),
            dma((bits, groups)),
            dma,
            dma,
        ],
        compiler_params=pltpu.CompilerParams(
            collective_id=0, has_side_effects=True, vmem_limit_bytes=60 * 2**20
        ),
    )(queries, keys, values, level_pattern, level_weight, out_weight)


def on_device(dims, queries, keys, values, level_pattern, level_weight, out_weight):
    n = lax.axis_size("seq")
    tokens, width = queries.shape
    heads = width // HD
    bits = n.bit_length() - 1
    _, rows, full = out_weight.shape
    cols = full // 2
    fused = rows % 16 == 0
    if fused and len(dims) == 3 and cols % 1024 == 0:
        return planned(dims, queries, keys, values, level_pattern, level_weight, out_weight)
    groups = min(4, heads)
    tiles = cols // 128
    if len(dims) == 3:
        long = max(range(3), key=lambda i: dims[i][0])
        a, b = [i for i in range(3) if i != long]
        orders = [(long, a, b), (long, b, a), (a, b, long)]
        share = max(1, tiles * 3 // 8)
        sizes = [share, share, tiles - 2 * share]
    else:
        orders, sizes = [tuple(range(len(dims)))], [tiles]
    cuts, lo = [], 0
    for size in sizes:
        cuts.append((lo * 128, size * 128))
        lo += size
    events = schedule(dims, orders, cuts, n, heads, groups, fused)
    plan = (dims, orders, cuts, events, n, fused)
    bf16, f32 = jnp.bfloat16, jnp.float32
    any_spec = pl.BlockSpec(memory_space=pl.ANY)
    vmem_spec = pl.BlockSpec(memory_space=pltpu.VMEM)
    if fused:
        out_shape = pltpu.VMEM((tokens, cols), f32)
        out_specs = vmem_spec
    else:
        out_shape = [
            jax.ShapeDtypeStruct((2, tokens, width), bf16),
            jax.ShapeDtypeStruct((2, n, rows, cols), bf16),
        ]
        out_specs = [any_spec, any_spec]
    dma = pltpu.SemaphoreType.DMA
    result = pl.pallas_call(
        functools.partial(kernel, plan),
        out_shape=out_shape,
        in_specs=[any_spec] * 3 + [vmem_spec] * 2 + [any_spec],
        out_specs=out_specs,
        scratch_shapes=[
            pltpu.VMEM((tokens, width), bf16),
            pltpu.VMEM((tokens, width), bf16),
            pltpu.VMEM((tokens, width), bf16),
            pltpu.VMEM((1, rows, full), bf16),
            pltpu.VMEM((2, n, rows, cols), bf16),
            pltpu.VMEM((2, tokens, width), bf16),
            pltpu.VMEM((tokens, width), f32),
            pltpu.VMEM((heads, HD, HD), f32),
            pltpu.VMEM((bits, heads, HD, HD), bf16),
            pltpu.VMEM((bits, heads, HD, HD), bf16),
            pltpu.VMEM((bits + 1, tokens, HD), f32),
            dma((4,)),
            dma,
            dma,
            dma,
            dma((len(orders), n if fused else 1, 2 * len(dims))),
            dma((len(orders), n)),
            dma((bits, groups)),
            dma((bits, groups)),
            dma((groups,)),
            dma((groups,)),
        ],
        compiler_params=pltpu.CompilerParams(
            collective_id=0, has_side_effects=True, vmem_limit_bytes=60 * 2**20
        ),
    )(queries, keys, values, level_pattern, level_weight, out_weight)
    if fused:
        return result
    att, gathered = result
    return jnp.einsum(
        "gtk,gkd->td", att, gathered.reshape(2, n * rows, cols), preferred_element_type=f32
    )


def solution(mesh):
    placed = (
        P("seq", "head"),
        P("seq", "head"),
        P("seq", "head"),
        P("seq"),
        P(),
        P("head", "seq", None),
    )
    return jax.shard_map(
        functools.partial(on_device, line_dims(mesh)),
        mesh=mesh, in_specs=placed, out_specs=P("seq", "head"), check_vma=False,
    )
```

```python
import functools
import itertools
import math

import jax
import jax.numpy as jnp
from jax import lax
from jax.experimental import pallas as pl
from jax.experimental.pallas import tpu as pltpu
from jax.sharding import PartitionSpec as P

HD = 128
MESH = pl.DeviceIdType.MESH
ORDER = (13, 16, 12, 7, 4, 18, 6, 17, 0, 15, 19, 10, 25, 3, 22, 9, 27, 21, 20, 23, 11, 79, 5, 30, 29, 24, 31, 91, 49, 8, 64, 2, 26, 128, 53, 94, 34, 32, 122, 1, 109, 28, 61, 35, 113, 33, 98, 66, 83, 92, 121, 107, 39, 80, 124, 51, 77, 65, 68, 57, 130, 54, 62, 14, 38, 132, 95, 115, 81, 76, 47, 36, 129, 37, 87, 46, 43, 117, 134, 40, 52, 102, 67, 133, 72, 69, 44, 106, 70, 41, 123, 42, 103, 84, 55, 96, 59, 74, 119, 89, 88, 45, 118, 82, 131, 93, 108, 100, 111, 78, 116, 104, 85, 114, 125, 63, 97, 126, 99, 90, 86, 58, 48, 135, 50, 73, 120, 75, 56, 60, 127, 101, 110, 112, 105, 71,)
LENGTHS = [4, 2, 2]
LAG = 6


def line_dims(mesh):
    n = mesh.shape["seq"]
    devices = mesh.devices.reshape(n, -1)[:, 0]
    coords = [tuple(getattr(d, "coords", ())) for d in devices]
    dims = []
    if len(set(coords)) == n:
        for axis in range(len(coords[0])):
            seen = [c[axis] - coords[0][axis] for c in coords]
            length = max(seen) + 1
            if length > 1:
                dims.append((length, seen.index(1)))
    stride = 1
    for length, step in sorted(dims, key=lambda d: d[1]):
        if step != stride:
            break
        stride *= length
    if not dims or stride != n:
        dims = [(2, 1 << i) for i in range(n.bit_length() - 1)]
    return sorted(dims, key=lambda d: -d[1])


def nearest(k, p, n):
    m = jnp.minimum(p, n - 1 - p)
    sign = jnp.where(p == m, 1, -1)
    near = (k + 1) // 2 * (2 * (k % 2) - 1)
    if n == 2:
        return p + k * (1 - 2 * p)
    return jnp.where(k <= 2 * m, p + near, p + sign * (k - m))


def kernel(
    plan, q_hbm, k_hbm, v_hbm, pattern_ref, table_ref, w_hbm, *rest
):
    dims, orders, cuts, events, n, fused = plan
    if fused:
        out_ref, *rest = rest
    else:
        att_hbm, w_out_hbm, *rest = rest
    (q_ref, k_ref, v_ref, w_ref, wbuf, att, acc, sub, outgoing, incoming, mixb,
     load_sem, own_sem, pair_send, pair_recv, w_send, w_recv, s_send, s_recv, a_send, a_recv) = rest
    me = lax.axis_index("seq")
    core = lax.axis_index("head")
    other = 1 - core
    tokens, width = q_ref.shape
    heads = width // HD
    cols = wbuf.shape[-1]
    bits = n.bit_length() - 1
    groups = a_send.shape[0]
    per = heads // groups
    place = [me // stride % length for length, stride in dims]

    loads = [
        pltpu.make_async_copy(src, dst, load_sem.at[i])
        for i, (src, dst) in enumerate(((w_hbm, w_ref), (k_hbm, k_ref), (v_hbm, v_ref), (q_hbm, q_ref)))
    ]
    for load in loads:
        load.start()

    barrier = pltpu.get_barrier_semaphore()
    total = 1
    pl.semaphore_signal(barrier, inc=1, device_id=(me, other), device_id_type=MESH)
    for bit in range(bits):
        pl.semaphore_signal(barrier, inc=1, device_id=(me ^ (1 << bit), core), device_id_type=MESH)
        total += 1
    for (length, stride), p in zip(dims, place):
        if length == 2:
            continue
        for step in (-1, 1):
            there = jnp.logical_and(p + step >= 0, p + step < length)

            @pl.when(there)
            def _():
                pl.semaphore_signal(barrier, inc=1, device_id=(me + step * stride, core), device_id_type=MESH)

            total = total + there.astype(jnp.int32)

    for l in range(bits + 1):
        if l == 0:
            ids = lax.broadcasted_iota(jnp.int32, (table_ref.shape[0], tokens), 0)
            one_hot = (ids == pattern_ref[...].reshape(1, tokens)).astype(jnp.float32)
            mix = lax.dot_general(
                one_hot, table_ref[...], (((0,), (0,)), ((), ())),
                precision=lax.Precision.HIGHEST, preferred_element_type=jnp.float32,
            )
        factor = 1.0 / math.sqrt(tokens * (1 if l == 0 else 2 ** (l - 1)))
        mixb[l] = jnp.broadcast_to(mix[:, l : l + 1] * factor, (tokens, HD))

    def head_cols(h):
        return slice(h * HD, (h + 1) * HD)

    loads[1].wait()
    loads[2].wait()

    def make_states(h):
        state = lax.dot_general(
            k_ref[:, head_cols(h)], v_ref[:, head_cols(h)], (((0,), (0,)), ((), ())),
            preferred_element_type=jnp.float32,
        )
        sub[h] = state
        outgoing[0, h] = state.astype(jnp.bfloat16)

    for h in range(heads):
        make_states(h)
    loads[0].wait()
    pl.semaphore_wait(barrier, total)

    def pair_copy():
        return pltpu.make_async_remote_copy(
            src_ref=w_ref.at[0, :, pl.ds(pl.multiple_of(other * cols, 128), cols)],
            dst_ref=wbuf.at[core, me], send_sem=pair_send, recv_sem=pair_recv,
            device_id=(me, other), device_id_type=MESH,
        )

    def pair_landed():
        return pltpu.make_async_remote_copy(
            src_ref=w_ref.at[0, :, pl.ds(pl.multiple_of(other * cols, 128), cols)],
            dst_ref=wbuf.at[other, me], send_sem=pair_send, recv_sem=pair_recv,
            device_id=(me, other), device_id_type=MESH,
        )

    pair_copy().start()
    own = pltpu.make_async_copy(
        w_ref.at[0, :, pl.ds(pl.multiple_of(core * cols, 128), cols)], wbuf.at[core, me], own_sem
    )
    own.start()

    def state_copy(level, group):
        piece = pl.ds(group * per, per)
        return pltpu.make_async_remote_copy(
            src_ref=outgoing.at[level, piece], dst_ref=incoming.at[level, piece],
            send_sem=s_send.at[level, group], recv_sem=s_recv.at[level, group],
            device_id=(me ^ (1 << level), core), device_id_type=MESH,
        )

    def sum_needed(level):
        return me // 2 ** (level + 1) != n // 2 ** (level + 1) - 1

    def active(level):
        return me // 2**level % 2 == 1

    def sends(level):
        return jnp.logical_or(jnp.logical_not(active(level)), sum_needed(level))

    def receives(level):
        return jnp.logical_or(active(level), sum_needed(level))

    for group in range(groups):
        @pl.when(sends(0))
        def _():
            state_copy(0, group).start()

    def weight_copy(part, source, slot, target):
        lo, size = cuts[part]
        piece = wbuf.at[:, source, :, pl.ds(lo, size)]
        return pltpu.make_async_remote_copy(
            src_ref=piece, dst_ref=piece,
            send_sem=w_send.at[part, source if fused else 0, slot], recv_sem=w_recv.at[part, source],
            device_id=(target, core), device_id_type=MESH,
        )

    def forward(part, source, at, arrived, action):
        order = orders[part]
        for rank in range(max(arrived, 0), len(order)):
            d = order[rank]
            length, stride = dims[d]
            for slot, step in ((2 * rank, 1), (2 * rank + 1, -1)):
                if rank == arrived and length == 2:
                    continue
                ok = jnp.logical_and(place[d] + step >= 0, place[d] + step < length)
                if rank == arrived:
                    ok = jnp.logical_and(ok, (place[d] - at[d]) * step > 0)

                @pl.when(ok)
                def _():
                    copy = weight_copy(part, source, slot, me + step * stride)
                    if action == "start":
                        copy.start()
                    else:
                        copy.wait_send()

    def source_of(part, ks):
        at = {d: nearest(k, place[d], dims[d][0]) for d, k in zip(orders[part], ks)}
        return at, sum(at[d] * dims[d][1] for d in at)

    def arrived_by(ks):
        return max((r for r, k in enumerate(ks) if k), default=-1)

    def weight_event(part, ks, arrived):
        at, source = source_of(part, ks)
        weight_copy(part, source, 0, me).wait_recv()
        forward(part, source, at, arrived, "start")
        if not fused:
            forward(part, source, at, arrived, "wait")

    def read_state(level, h):
        acc[:, head_cols(h)] += mixb[level + 1] * jnp.dot(
            q_ref[:, head_cols(h)], incoming[level, h], preferred_element_type=jnp.float32
        )

    def within_event(h):
        columns = head_cols(h)
        scores = lax.dot_general(
            q_ref[:, columns], k_ref[:, columns], (((1,), (1,)), ((), ())),
            preferred_element_type=jnp.float32,
        )
        row = lax.broadcasted_iota(jnp.int32, (tokens, tokens), 0)
        col = lax.broadcasted_iota(jnp.int32, (tokens, tokens), 1)
        inner = jnp.where(col <= row, scores, 0.0).astype(jnp.bfloat16)
        acc[:, columns] = mixb[0] * jnp.dot(inner, v_ref[:, columns], preferred_element_type=jnp.float32)

    def att_copy(group, mine):
        columns = pl.ds(group * per * HD, per * HD)
        which = core if mine else other
        return pltpu.make_async_remote_copy(
            src_ref=att.at[core, :, columns], dst_ref=att.at[which, :, columns],
            send_sem=a_send.at[group], recv_sem=a_recv.at[group],
            device_id=(me, other), device_id_type=MESH,
        )

    def state_event(level, group):
        @pl.when(receives(level))
        def _():
            state_copy(level, group).wait_recv()

        span = range(group * per, (group + 1) * per)
        if level + 1 < bits:
            @pl.when(sum_needed(level))
            def _():
                for h in span:
                    summed = sub[h] + incoming[level, h].astype(jnp.float32)
                    sub[h] = summed
                    outgoing[level + 1, h] = summed.astype(jnp.bfloat16)

            @pl.when(sends(level + 1))
            def _():
                state_copy(level + 1, group).start()

        @pl.when(active(level))
        def _():
            for h in span:
                read_state(level, h)

        if level + 1 == bits:
            columns = slice(group * per * HD, (group + 1) * per * HD)
            att[core, :, columns] = acc[:, columns].astype(jnp.bfloat16)
            att_copy(group, True).start()

    own.wait()
    pair_landed().wait_recv()
    for part in range(len(orders)):
        at, source = source_of(part, (0,) * len(dims))
        forward(part, source, at, -1, "start")
        if not fused:
            forward(part, source, at, -1, "wait")
    loads[3].wait()

    def project(part):
        lo, size = cuts[part]
        columns = slice(lo, lo + size)
        flat = [wbuf[g, :, :, columns].reshape(-1, size) for g in range(2)]
        out_ref[:, columns] = jnp.dot(att[0], flat[0], preferred_element_type=jnp.float32) + jnp.dot(
            att[1], flat[1], preferred_element_type=jnp.float32
        )

    for event in events:
        if event[0] == "within":
            within_event(event[1])
        elif event[0] == "state":
            state_event(event[1], event[2])
        elif event[0] == "weight":
            weight_event(*event[1:])
        elif event[0] == "loop":
            lengths = [[dims[d][0] for d in order] for order in orders]

            def each(e, carry):
                for part, order in enumerate(orders):
                    for arrived in range(len(order)):
                        below = math.prod(lengths[part][:arrived])
                        ks = []
                        rest_e = e
                        for length in lengths[part]:
                            ks.append(rest_e % length)
                            rest_e = rest_e // length

                        @pl.when(jnp.logical_and(e >= below, e < below * lengths[part][arrived]))
                        def _():
                            weight_event(part, ks, arrived)

                return carry

            lax.fori_loop(1, n, each, 0)
        elif event[0] == "att":
            for group in range(groups):
                att_copy(group, False).wait_recv()
        elif event[0] == "project" and fused:
            project(event[1])

    def finish(part, e):
        ks = []
        for d in orders[part]:
            ks.append(e % dims[d][0])
            e = e // dims[d][0]
        return ks

    pair_copy().wait_send()
    for group in range(groups):
        att_copy(group, True).wait_send()
        for level in range(bits):
            @pl.when(sends(level))
            def _():
                state_copy(level, group).wait_send()
    if fused:
        for part in range(len(orders)):
            for e in range(n):
                ks = finish(part, e)
                at, source = source_of(part, ks)
                forward(part, source, at, arrived_by(ks), "wait")
    if not fused:
        stores = [pltpu.make_async_copy(att, att_hbm, load_sem.at[0]), pltpu.make_async_copy(wbuf, w_out_hbm, load_sem.at[1])]
        for store in stores:
            store.start()
        for store in stores:
            store.wait()


def schedule(dims, orders, cuts, n, heads, groups, unrolled):
    bits = n.bit_length() - 1
    whole = sum(size for _, size in cuts)
    timed = []
    for h in range(heads):
        timed.append((0.35 * h / heads, ("within", h)))
    for level in range(bits):
        for group in range(groups):
            timed.append((0.45 + 0.75 * level + 0.25 * group, ("state", level, group)))
    if not unrolled:
        tail = [("loop",), ("att",)]
    else:
        last = {}
        for part, order in enumerate(orders):
            lengths = [dims[d][0] for d in order]
            count = [0] * len(order)
            for rev in itertools.product(*[range(length) for length in lengths[::-1]]):
                ks = rev[::-1]
                arrived = max((r for r, k in enumerate(ks) if k), default=-1)
                if arrived < 0:
                    continue
                count[arrived] += 1
                when = count[arrived] * cuts[part][1] / whole * 1.8 + 0.3 * sum(1 for k in ks if k)
                if arrived == len(order) - 1 and lengths[-1] == 2:
                    when += 100
                timed.append((when, ("weight", part, ks, arrived)))
        tail = [("att",)]
    timed.sort(key=lambda t: t[0])
    return [e for _, e in timed] + tail + [("project", p) for p in range(len(orders))]


def planned_kernel(
    plan, q_hbm, k_hbm, v_hbm, pattern_ref, table_ref, w_hbm, out_ref,
    q_ref, k_ref, v_ref, w_ref, wbuf, att, acc, sub, outgoing, incoming, mixb,
    load_sem, own_sem, pair_send, pair_recv, w_send, w_recv, s_send, s_recv, a_send, a_recv,
):
    dims, parts, events, n = plan
    me = lax.axis_index("seq")
    core = lax.axis_index("head")
    other = 1 - core
    tokens, width = q_ref.shape
    rows = w_ref.shape[1]
    heads = width // HD
    cols = wbuf.shape[-1]
    bits = n.bit_length() - 1
    groups = s_recv.shape[1]
    per = heads // groups
    place = [me // stride % length for length, stride in dims]

    loads = {
        name: pltpu.make_async_copy(src, dst, load_sem.at[i])
        for i, (name, src, dst) in enumerate(
            (("w", w_hbm, w_ref), ("k", k_hbm, k_ref), ("v", v_hbm, v_ref), ("q", q_hbm, q_ref))
        )
    }
    for load in loads.values():
        load.start()

    barrier = pltpu.get_barrier_semaphore()
    total = 1
    pl.semaphore_signal(barrier, inc=1, device_id=(me, other), device_id_type=MESH)
    for (length, stride), p in zip(dims, place):
        for step in (-1, 1):
            there = jnp.logical_and(p + step >= 0, p + step < length)

            @pl.when(there)
            def _():
                for c in range(2):
                    pl.semaphore_signal(barrier, inc=1, device_id=(me + step * stride, c), device_id_type=MESH)

            total = total + 2 * there.astype(jnp.int32)
    for bit in range(bits - 1):
        if all(1 << bit != stride for _, stride in dims):
            pl.semaphore_signal(barrier, inc=1, device_id=(me ^ (1 << bit), core), device_id_type=MESH)
            total = total + 1

    waited = set()

    def loaded(*names):
        for name in names:
            if name not in waited:
                waited.add(name)
                loads[name].wait()

    loaded("w")
    pl.semaphore_wait(barrier, total)

    def head_cols(h):
        return slice(h * HD, (h + 1) * HD)

    def pair_copy(which):
        return pltpu.make_async_remote_copy(
            src_ref=w_ref.at[0, :, pl.ds(pl.multiple_of(other * cols, 128), cols)],
            dst_ref=wbuf.at[which, me], send_sem=pair_send, recv_sem=pair_recv,
            device_id=(me, other), device_id_type=MESH,
        )

    own = pltpu.make_async_copy(
        w_ref.at[0, :, pl.ds(pl.multiple_of(core * cols, 128), cols)], wbuf.at[core, me], own_sem
    )

    top = bits - 1
    reach, climb = dims[0]

    def state_copy(level, group, relay=False):
        piece = pl.ds(group * per, per)
        target = me + climb if level == top else me ^ (1 << level)
        return pltpu.make_async_remote_copy(
            src_ref=(incoming if relay else outgoing).at[level, piece], dst_ref=incoming.at[level, piece],
            send_sem=s_send.at[level], recv_sem=s_recv.at[level, group],
            device_id=(target, core), device_id_type=MESH,
        )

    def sum_needed(level, who=me):
        if level == top - 1:
            return who // climb == reach // 2 - 1
        return who // 2 ** (level + 1) != n // 2 ** (level + 1) - 1

    def active(level, who=me):
        return who // 2**level % 2 == 1

    def receives(level, who=me):
        if level == top:
            return active(level, who)
        return jnp.logical_or(active(level, who), sum_needed(level, who))

    def sends(level):
        if level == top:
            return place[0] == reach // 2 - 1
        return receives(level, me ^ (1 << level))

    relays = jnp.logical_and(active(top), place[0] < reach - 1)

    def first_copy(part, slot, target, half):
        g, lo, size, _ = parts[part]
        return pltpu.make_async_remote_copy(
            src_ref=w_ref.at[0, :, pl.ds(half * cols + lo, size)],
            dst_ref=wbuf.at[g, me, :, pl.ds(lo, size)],
            send_sem=w_send.at[part, slot], recv_sem=w_recv.at[part, me],
            device_id=(target, half), device_id_type=MESH,
        )

    def first(part, ranks):
        g, _, _, order = parts[part]
        for rank in ranks:
            d = order[rank]
            length, stride = dims[d]
            for slot, step in ((2 * rank, 1), (2 * rank + 1, -1)):
                ok = jnp.logical_and(place[d] + step >= 0, place[d] + step < length)

                @pl.when(jnp.logical_and(ok, core == g))
                def _():
                    for half in range(2):
                        first_copy(part, slot, me + step * stride, half).start()

    def weight_copy(part, source, slot, target):
        g, lo, size, _ = parts[part]
        piece = wbuf.at[g, source, :, pl.ds(lo, size)]
        return pltpu.make_async_remote_copy(
            src_ref=piece, dst_ref=piece,
            send_sem=w_send.at[part, slot], recv_sem=w_recv.at[part, source],
            device_id=(target, core), device_id_type=MESH,
        )

    def forward(part, ks):
        order = parts[part][3]
        at = {d: nearest(k, place[d], dims[d][0]) for d, k in zip(order, ks)}
        source = sum(at[d] * dims[d][1] for d in at)
        arrived = max(r for r, k in enumerate(ks) if k)
        weight_copy(part, source, 0, me).wait_recv()
        for rank in range(arrived, len(order)):
            d = order[rank]
            length, stride = dims[d]
            for slot, step in ((2 * rank, 1), (2 * rank + 1, -1)):
                if rank == arrived and length == 2:
                    continue
                ok = jnp.logical_and(place[d] + step >= 0, place[d] + step < length)
                if rank == arrived:
                    ok = jnp.logical_and(ok, (place[d] - at[d]) * step > 0)

                @pl.when(ok)
                def _():
                    weight_copy(part, source, slot, me + step * stride).start()

    def sent(part):
        g, lo, size, order = parts[part]
        ahead = 1
        for rank, d in enumerate(order):
            length = dims[d][0]
            for slot, up in ((2 * rank, True), (2 * rank + 1, False)):
                for p in range(length - 1) if up else range(1, length):
                    count = ahead - 1 + ahead * (p if up else length - 1 - p)
                    for mine in (0, 2):
                        if count + mine == 0:
                            continue

                        @pl.when(jnp.logical_and(place[d] == p, (core == g) == (mine == 2)))
                        def _():
                            piece = wbuf.at[g, pl.ds(0, count + mine), :, pl.ds(lo, size)]
                            pltpu.make_async_remote_copy(
                                src_ref=piece, dst_ref=piece, send_sem=w_send.at[part, slot], recv_sem=w_recv.at[part, 0],
                                device_id=(me, other), device_id_type=MESH,
                            ).wait_send()

            ahead *= length

    def make_mix():
        ids = lax.broadcasted_iota(jnp.int32, (table_ref.shape[0], tokens), 0)
        one_hot = (ids == pattern_ref[...].reshape(1, tokens)).astype(jnp.float32)
        mix = lax.dot_general(
            one_hot, table_ref[...], (((0,), (0,)), ((), ())),
            precision=lax.Precision.HIGHEST, preferred_element_type=jnp.float32,
        )
        for l in range(bits + 1):
            factor = 1.0 / math.sqrt(tokens * (1 if l == 0 else 2 ** (l - 1)))
            mixb[l] = jnp.broadcast_to(mix[:, l : l + 1] * factor, (tokens, HD))

    def state_start(group):
        loaded("k", "v")
        for h in range(group * per, (group + 1) * per):
            state = lax.dot_general(
                k_ref[:, head_cols(h)], v_ref[:, head_cols(h)], (((0,), (0,)), ((), ())),
                preferred_element_type=jnp.float32,
            )
            sub[h] = state
            outgoing[0, h] = state.astype(jnp.bfloat16)

        @pl.when(sends(0))
        def _():
            state_copy(0, group).start()

    def within_event(h):
        columns = head_cols(h)
        scores = lax.dot_general(
            q_ref[:, columns], k_ref[:, columns], (((1,), (1,)), ((), ())),
            preferred_element_type=jnp.float32,
        )
        row = lax.broadcasted_iota(jnp.int32, (tokens, tokens), 0)
        col = lax.broadcasted_iota(jnp.int32, (tokens, tokens), 1)
        inner = jnp.where(col <= row, scores, 0.0).astype(jnp.bfloat16)
        acc[:, columns] = mixb[0] * jnp.dot(inner, v_ref[:, columns], preferred_element_type=jnp.float32)

    def att_copy(group):
        columns = pl.ds(group * per * HD, per * HD)
        return pltpu.make_async_remote_copy(
            src_ref=att.at[core, :, columns], dst_ref=att.at[core, :, columns],
            send_sem=a_send, recv_sem=a_recv,
            device_id=(me, other), device_id_type=MESH,
        )

    def att_whole(which):
        return pltpu.make_async_remote_copy(
            src_ref=att.at[which], dst_ref=att.at[which], send_sem=a_send, recv_sem=a_recv,
            device_id=(me, other), device_id_type=MESH,
        )

    def state_event(level, group):
        @pl.when(receives(level))
        def _():
            state_copy(level, group).wait_recv()

        span = range(group * per, (group + 1) * per)
        if level + 1 < bits:
            @pl.when(sum_needed(level))
            def _():
                for h in span:
                    summed = sub[h] + incoming[level, h].astype(jnp.float32)
                    sub[h] = summed
                    outgoing[level + 1, h] = summed.astype(jnp.bfloat16)

            @pl.when(sends(level + 1))
            def _():
                state_copy(level + 1, group).start()
        else:
            @pl.when(relays)
            def _():
                state_copy(level, group, True).start()

    def read_event(level, group):
        @pl.when(active(level))
        def _():
            for h in range(group * per, (group + 1) * per):
                acc[:, head_cols(h)] += mixb[level + 1] * jnp.dot(
                    q_ref[:, head_cols(h)], incoming[level, h], preferred_element_type=jnp.float32
                )

        if level + 1 == bits:
            columns = slice(group * per * HD, (group + 1) * per * HD)
            att[core, :, columns] = acc[:, columns].astype(jnp.bfloat16)
            att_copy(group).start()

    def project(part, k):
        g, lo, size, _ = parts[part]
        length, stride = dims[0]
        slab = nearest(k, place[0], length) * stride
        depth = stride * rows
        piece = wbuf[g, pl.ds(slab, stride), :, lo : lo + size].reshape(depth, size)
        taken = att[g, :, pl.ds(pl.multiple_of(slab * rows, math.gcd(depth, 1024)), depth)]
        out_ref[:, lo : lo + size] += jnp.dot(taken, piece, preferred_element_type=jnp.float32)

    for event in events:
        kind, args = event[0], event[1:]
        if kind == "first":
            first(*args)
        elif kind == "pair":
            pair_copy(core).start()
            own.start()
        elif kind == "paired":
            own.wait()
            pair_copy(other).wait_recv()
        elif kind == "start":
            state_start(*args)
        elif kind == "mix":
            make_mix()
            out_ref[...] = jnp.zeros_like(out_ref)
        elif kind == "within":
            loaded("k", "v", "q")
            within_event(*args)
        elif kind == "state":
            state_event(*args)
        elif kind == "read":
            read_event(*args)
        elif kind == "weight":
            forward(*args)
        elif kind == "att":
            att_whole(other).wait_recv()
        elif kind == "project":
            project(*args)

    pair_copy(core).wait_send()
    att_whole(core).wait_send()
    for level in range(bits):
        @pl.when(jnp.logical_or(sends(level), relays) if level == top else sends(level))
        def _():
            pltpu.make_async_remote_copy(
                src_ref=outgoing.at[level], dst_ref=incoming.at[level],
                send_sem=s_send.at[level], recv_sem=s_recv.at[level, 0],
                device_id=(me ^ (1 << level), core), device_id_type=MESH,
            ).wait_send()
    for part in range(len(parts)):
        sent(part)


def make_parts(dims, tiles):
    long = max(range(3), key=lambda i: dims[i][0])
    a, b = [i for i in range(3) if i != long]
    direct = max(1, tiles // 8)
    most = (tiles - direct + 1) // 2
    parts = []
    for g, sizes in enumerate(((most, tiles - direct - most, direct), (tiles - direct - most, most, direct))):
        last = (b, a, long) if g == 0 else (a, b, long)
        lo = 0
        for size, order in zip(sizes, ((long, b, a), (long, a, b), last)):
            parts.append((g, lo * 128, size * 128, order))
            lo += size
    return parts


def make_events(dims, parts, n, heads, groups):
    bits = n.bit_length() - 1
    timed = []
    for part, (_, _, _, order) in enumerate(parts):
        for rank, d in enumerate(order):
            timed.append(((0, rank, part), ("first", part, (rank,))))
    for group in range(groups):
        timed.append(((1, group), ("start", group)))
    for h in range(heads):
        timed.append(((3 + h, 9), ("within", h)))
    for level in range(bits):
        for group in range(groups):
            timed.append(((3 + 3 * level + group, 0), ("state", level, group)))
    for part, (_, _, _, order) in enumerate(parts):
        for ks in itertools.product(*[range(dims[d][0]) for d in order]):
            if any(ks):
                timed.append(((3 * sum(1 for k in ks if k) + sum(ks), part), ("weight", part, ks)))
    if ORDER and len(ORDER) == len(timed) and [d[0] for d in dims] == LENGTHS:
        chosen = [timed[i][1] for i in ORDER]
    else:
        chosen = [event for _, event in sorted(timed, key=lambda t: t[0])]
    events, inside = [], []
    for event in chosen:
        if event[0] == "within" and event[1] in inside:
            continue
        due = [event[1]] if event[0] == "within" else []
        if event[0] == "state":
            events.append(event)
            per = heads // groups
            due = [h for h in range(event[2] * per, (event[2] + 1) * per) if h not in inside]
        if due and not inside:
            events.append(("mix",))
        events += [("within", h) for h in due]
        inside += due
        if event[0] == "state":
            events.append(("read",) + event[1:])
        elif event[0] != "within":
            events.append(event)
    at = 1 + max(i for i, e in enumerate(events) if e[0] == "start")
    events.insert(at, ("pair",))
    reads = max(i for i, e in enumerate(events) if e[0] == "read")
    at = min(len(events), reads + 1 + LAG)
    events[at:at] = [("paired",), ("att",)]
    ready = {}
    for i, e in enumerate(events):
        if e[0] == "weight":
            key = (e[1], e[2][parts[e[1]][3].index(0)])
            ready[key] = max(ready.get(key, at + 1), i)
    placed, queue = [], []
    for i, e in enumerate(events):
        placed.append(e)
        queue += sorted((key for key, j in ready.items() if j == i), key=lambda key: key[::-1])
        if queue and i + 1 < len(events):
            placed.append(("project",) + queue.pop(0))
    placed += [("project",) + key for key in queue]
    return placed


def planned(dims, queries, keys, values, level_pattern, level_weight, out_weight):
    n = lax.axis_size("seq")
    tokens, width = queries.shape
    heads = width // HD
    bits = n.bit_length() - 1
    _, rows, full = out_weight.shape
    cols = full // 2
    groups = min(4, heads)
    parts = make_parts(dims, cols // 128)
    events = make_events(dims, parts, n, heads, groups)
    bf16, f32 = jnp.bfloat16, jnp.float32
    any_spec = pl.BlockSpec(memory_space=pl.ANY)
    vmem_spec = pl.BlockSpec(memory_space=pltpu.VMEM)
    dma = pltpu.SemaphoreType.DMA
    return pl.pallas_call(
        functools.partial(planned_kernel, (dims, parts, events, n)),
        out_shape=pltpu.VMEM((tokens, cols), f32),
        in_specs=[any_spec] * 3 + [vmem_spec] * 2 + [any_spec],
        out_specs=vmem_spec,
        scratch_shapes=[
            pltpu.VMEM((tokens, width), bf16),
            pltpu.VMEM((tokens, width), bf16),
            pltpu.VMEM((tokens, width), bf16),
            pltpu.VMEM((1, rows, full), bf16),
            pltpu.VMEM((2, n, rows, cols), bf16),
            pltpu.VMEM((2, tokens, width), bf16),
            pltpu.VMEM((tokens, width), f32),
            pltpu.VMEM((heads, HD, HD), f32),
            pltpu.VMEM((bits, heads, HD, HD), bf16),
            pltpu.VMEM((bits, heads, HD, HD), bf16),
            pltpu.VMEM((bits + 1, tokens, HD), f32),
            dma((4,)),
            dma,
            dma,
            dma,
            dma((len(parts), 2 * len(dims))),
            dma((len(parts), n)),
            dma((bits,)),
            dma((bits, groups)),
            dma,
            dma,
        ],
        compiler_params=pltpu.CompilerParams(
            collective_id=0, has_side_effects=True, vmem_limit_bytes=60 * 2**20
        ),
    )(queries, keys, values, level_pattern, level_weight, out_weight)


def on_device(dims, queries, keys, values, level_pattern, level_weight, out_weight):
    n = lax.axis_size("seq")
    tokens, width = queries.shape
    heads = width // HD
    bits = n.bit_length() - 1
    _, rows, full = out_weight.shape
    cols = full // 2
    fused = rows % 16 == 0
    if fused and len(dims) == 3 and cols % 1024 == 0:
        return planned(dims, queries, keys, values, level_pattern, level_weight, out_weight)
    groups = min(4, heads)
    tiles = cols // 128
    if len(dims) == 3:
        long = max(range(3), key=lambda i: dims[i][0])
        a, b = [i for i in range(3) if i != long]
        orders = [(long, a, b), (long, b, a), (a, b, long)]
        share = max(1, tiles * 3 // 8)
        sizes = [share, share, tiles - 2 * share]
    else:
        orders, sizes = [tuple(range(len(dims)))], [tiles]
    cuts, lo = [], 0
    for size in sizes:
        cuts.append((lo * 128, size * 128))
        lo += size
    events = schedule(dims, orders, cuts, n, heads, groups, fused)
    plan = (dims, orders, cuts, events, n, fused)
    bf16, f32 = jnp.bfloat16, jnp.float32
    any_spec = pl.BlockSpec(memory_space=pl.ANY)
    vmem_spec = pl.BlockSpec(memory_space=pltpu.VMEM)
    if fused:
        out_shape = pltpu.VMEM((tokens, cols), f32)
        out_specs = vmem_spec
    else:
        out_shape = [
            jax.ShapeDtypeStruct((2, tokens, width), bf16),
            jax.ShapeDtypeStruct((2, n, rows, cols), bf16),
        ]
        out_specs = [any_spec, any_spec]
    dma = pltpu.SemaphoreType.DMA
    result = pl.pallas_call(
        functools.partial(kernel, plan),
        out_shape=out_shape,
        in_specs=[any_spec] * 3 + [vmem_spec] * 2 + [any_spec],
        out_specs=out_specs,
        scratch_shapes=[
            pltpu.VMEM((tokens, width), bf16),
            pltpu.VMEM((tokens, width), bf16),
            pltpu.VMEM((tokens, width), bf16),
            pltpu.VMEM((1, rows, full), bf16),
            pltpu.VMEM((2, n, rows, cols), bf16),
            pltpu.VMEM((2, tokens, width), bf16),
            pltpu.VMEM((tokens, width), f32),
            pltpu.VMEM((heads, HD, HD), f32),
            pltpu.VMEM((bits, heads, HD, HD), bf16),
            pltpu.VMEM((bits, heads, HD, HD), bf16),
            pltpu.VMEM((bits + 1, tokens, HD), f32),
            dma((4,)),
            dma,
            dma,
            dma,
            dma((len(orders), n if fused else 1, 2 * len(dims))),
            dma((len(orders), n)),
            dma((bits, groups)),
            dma((bits, groups)),
            dma((groups,)),
            dma((groups,)),
        ],
        compiler_params=pltpu.CompilerParams(
            collective_id=0, has_side_effects=True, vmem_limit_bytes=60 * 2**20
        ),
    )(queries, keys, values, level_pattern, level_weight, out_weight)
    if fused:
        return result
    att, gathered = result
    return jnp.einsum(
        "gtk,gkd->td", att, gathered.reshape(2, n * rows, cols), preferred_element_type=f32
    )


def solution(mesh):
    placed = (
        P("seq", "head"),
        P("seq", "head"),
        P("seq", "head"),
        P("seq"),
        P(),
        P("head", "seq", None),
    )
    return jax.shard_map(
        functools.partial(on_device, line_dims(mesh)),
        mesh=mesh, in_specs=placed, out_specs=P("seq", "head"), check_vma=False,
    )
```

```python
import functools
import itertools
import math

import jax
import jax.numpy as jnp
from jax import lax
from jax.experimental import pallas as pl
from jax.experimental.pallas import tpu as pltpu
from jax.sharding import PartitionSpec as P

HD = 128
MESH = pl.DeviceIdType.MESH
ORDER = (3, 15, 10, 9, 11, 6, 12, 18, 20, 19, 29, 2, 26, 24, 21, 7, 23, 94, 0, 4, 17, 25, 28, 27, 22, 30, 14, 32, 16, 98, 13, 109, 113, 31, 83, 34, 49, 33, 95, 8, 92, 53, 64, 79, 128, 122, 38, 68, 36, 107, 77, 121, 102, 91, 117, 72, 124, 76, 35, 1, 51, 84, 129, 37, 5, 132, 40, 39, 123, 87, 62, 57, 42, 80, 114, 111, 100, 106, 108, 115, 69, 54, 134, 73, 104, 99, 41, 43, 66, 93, 88, 50, 47, 81, 133, 44, 45, 130, 125, 131, 119, 63, 96, 110, 59, 89, 90, 74, 135, 126, 55, 61, 78, 46, 101, 112, 82, 70, 85, 127, 105, 58, 67, 118, 65, 116, 120, 103, 48, 75, 60, 86, 52, 71, 56, 97,)
LENGTHS = [4, 2, 2]
LAG = 6


def line_dims(mesh):
    n = mesh.shape["seq"]
    devices = mesh.devices.reshape(n, -1)[:, 0]
    coords = [tuple(getattr(d, "coords", ())) for d in devices]
    dims = []
    if len(set(coords)) == n:
        for axis in range(len(coords[0])):
            seen = [c[axis] - coords[0][axis] for c in coords]
            length = max(seen) + 1
            if length > 1:
                dims.append((length, seen.index(1)))
    stride = 1
    for length, step in sorted(dims, key=lambda d: d[1]):
        if step != stride:
            break
        stride *= length
    if not dims or stride != n:
        dims = [(2, 1 << i) for i in range(n.bit_length() - 1)]
    return sorted(dims, key=lambda d: -d[1])


def nearest(k, p, n):
    m = jnp.minimum(p, n - 1 - p)
    sign = jnp.where(p == m, 1, -1)
    near = (k + 1) // 2 * (2 * (k % 2) - 1)
    if n == 2:
        return p + k * (1 - 2 * p)
    return jnp.where(k <= 2 * m, p + near, p + sign * (k - m))


def kernel(
    plan, q_hbm, k_hbm, v_hbm, pattern_ref, table_ref, w_hbm, *rest
):
    dims, orders, cuts, events, n, fused = plan
    if fused:
        out_ref, *rest = rest
    else:
        att_hbm, w_out_hbm, *rest = rest
    (q_ref, k_ref, v_ref, w_ref, wbuf, att, acc, sub, outgoing, incoming, mixb,
     load_sem, own_sem, pair_send, pair_recv, w_send, w_recv, s_send, s_recv, a_send, a_recv) = rest
    me = lax.axis_index("seq")
    core = lax.axis_index("head")
    other = 1 - core
    tokens, width = q_ref.shape
    heads = width // HD
    cols = wbuf.shape[-1]
    bits = n.bit_length() - 1
    groups = a_send.shape[0]
    per = heads // groups
    place = [me // stride % length for length, stride in dims]

    loads = [
        pltpu.make_async_copy(src, dst, load_sem.at[i])
        for i, (src, dst) in enumerate(((w_hbm, w_ref), (k_hbm, k_ref), (v_hbm, v_ref), (q_hbm, q_ref)))
    ]
    for load in loads:
        load.start()

    barrier = pltpu.get_barrier_semaphore()
    total = 1
    pl.semaphore_signal(barrier, inc=1, device_id=(me, other), device_id_type=MESH)
    for bit in range(bits):
        pl.semaphore_signal(barrier, inc=1, device_id=(me ^ (1 << bit), core), device_id_type=MESH)
        total += 1
    for (length, stride), p in zip(dims, place):
        if length == 2:
            continue
        for step in (-1, 1):
            there = jnp.logical_and(p + step >= 0, p + step < length)

            @pl.when(there)
            def _():
                pl.semaphore_signal(barrier, inc=1, device_id=(me + step * stride, core), device_id_type=MESH)

            total = total + there.astype(jnp.int32)

    for l in range(bits + 1):
        if l == 0:
            ids = lax.broadcasted_iota(jnp.int32, (table_ref.shape[0], tokens), 0)
            one_hot = (ids == pattern_ref[...].reshape(1, tokens)).astype(jnp.float32)
            mix = lax.dot_general(
                one_hot, table_ref[...], (((0,), (0,)), ((), ())),
                precision=lax.Precision.HIGHEST, preferred_element_type=jnp.float32,
            )
        factor = 1.0 / math.sqrt(tokens * (1 if l == 0 else 2 ** (l - 1)))
        mixb[l] = jnp.broadcast_to(mix[:, l : l + 1] * factor, (tokens, HD))

    def head_cols(h):
        return slice(h * HD, (h + 1) * HD)

    loads[1].wait()
    loads[2].wait()

    def make_states(h):
        state = lax.dot_general(
            k_ref[:, head_cols(h)], v_ref[:, head_cols(h)], (((0,), (0,)), ((), ())),
            preferred_element_type=jnp.float32,
        )
        sub[h] = state
        outgoing[0, h] = state.astype(jnp.bfloat16)

    for h in range(heads):
        make_states(h)
    loads[0].wait()
    pl.semaphore_wait(barrier, total)

    def pair_copy():
        return pltpu.make_async_remote_copy(
            src_ref=w_ref.at[0, :, pl.ds(pl.multiple_of(other * cols, 128), cols)],
            dst_ref=wbuf.at[core, me], send_sem=pair_send, recv_sem=pair_recv,
            device_id=(me, other), device_id_type=MESH,
        )

    def pair_landed():
        return pltpu.make_async_remote_copy(
            src_ref=w_ref.at[0, :, pl.ds(pl.multiple_of(other * cols, 128), cols)],
            dst_ref=wbuf.at[other, me], send_sem=pair_send, recv_sem=pair_recv,
            device_id=(me, other), device_id_type=MESH,
        )

    pair_copy().start()
    own = pltpu.make_async_copy(
        w_ref.at[0, :, pl.ds(pl.multiple_of(core * cols, 128), cols)], wbuf.at[core, me], own_sem
    )
    own.start()

    def state_copy(level, group):
        piece = pl.ds(group * per, per)
        return pltpu.make_async_remote_copy(
            src_ref=outgoing.at[level, piece], dst_ref=incoming.at[level, piece],
            send_sem=s_send.at[level, group], recv_sem=s_recv.at[level, group],
            device_id=(me ^ (1 << level), core), device_id_type=MESH,
        )

    def sum_needed(level):
        return me // 2 ** (level + 1) != n // 2 ** (level + 1) - 1

    def active(level):
        return me // 2**level % 2 == 1

    def sends(level):
        return jnp.logical_or(jnp.logical_not(active(level)), sum_needed(level))

    def receives(level):
        return jnp.logical_or(active(level), sum_needed(level))

    for group in range(groups):
        @pl.when(sends(0))
        def _():
            state_copy(0, group).start()

    def weight_copy(part, source, slot, target):
        lo, size = cuts[part]
        piece = wbuf.at[:, source, :, pl.ds(lo, size)]
        return pltpu.make_async_remote_copy(
            src_ref=piece, dst_ref=piece,
            send_sem=w_send.at[part, source if fused else 0, slot], recv_sem=w_recv.at[part, source],
            device_id=(target, core), device_id_type=MESH,
        )

    def forward(part, source, at, arrived, action):
        order = orders[part]
        for rank in range(max(arrived, 0), len(order)):
            d = order[rank]
            length, stride = dims[d]
            for slot, step in ((2 * rank, 1), (2 * rank + 1, -1)):
                if rank == arrived and length == 2:
                    continue
                ok = jnp.logical_and(place[d] + step >= 0, place[d] + step < length)
                if rank == arrived:
                    ok = jnp.logical_and(ok, (place[d] - at[d]) * step > 0)

                @pl.when(ok)
                def _():
                    copy = weight_copy(part, source, slot, me + step * stride)
                    if action == "start":
                        copy.start()
                    else:
                        copy.wait_send()

    def source_of(part, ks):
        at = {d: nearest(k, place[d], dims[d][0]) for d, k in zip(orders[part], ks)}
        return at, sum(at[d] * dims[d][1] for d in at)

    def arrived_by(ks):
        return max((r for r, k in enumerate(ks) if k), default=-1)

    def weight_event(part, ks, arrived):
        at, source = source_of(part, ks)
        weight_copy(part, source, 0, me).wait_recv()
        forward(part, source, at, arrived, "start")
        if not fused:
            forward(part, source, at, arrived, "wait")

    def read_state(level, h):
        acc[:, head_cols(h)] += mixb[level + 1] * jnp.dot(
            q_ref[:, head_cols(h)], incoming[level, h], preferred_element_type=jnp.float32
        )

    def within_event(h):
        columns = head_cols(h)
        scores = lax.dot_general(
            q_ref[:, columns], k_ref[:, columns], (((1,), (1,)), ((), ())),
            preferred_element_type=jnp.float32,
        )
        row = lax.broadcasted_iota(jnp.int32, (tokens, tokens), 0)
        col = lax.broadcasted_iota(jnp.int32, (tokens, tokens), 1)
        inner = jnp.where(col <= row, scores, 0.0).astype(jnp.bfloat16)
        acc[:, columns] = mixb[0] * jnp.dot(inner, v_ref[:, columns], preferred_element_type=jnp.float32)

    def att_copy(group, mine):
        columns = pl.ds(group * per * HD, per * HD)
        which = core if mine else other
        return pltpu.make_async_remote_copy(
            src_ref=att.at[core, :, columns], dst_ref=att.at[which, :, columns],
            send_sem=a_send.at[group], recv_sem=a_recv.at[group],
            device_id=(me, other), device_id_type=MESH,
        )

    def state_event(level, group):
        @pl.when(receives(level))
        def _():
            state_copy(level, group).wait_recv()

        span = range(group * per, (group + 1) * per)
        if level + 1 < bits:
            @pl.when(sum_needed(level))
            def _():
                for h in span:
                    summed = sub[h] + incoming[level, h].astype(jnp.float32)
                    sub[h] = summed
                    outgoing[level + 1, h] = summed.astype(jnp.bfloat16)

            @pl.when(sends(level + 1))
            def _():
                state_copy(level + 1, group).start()

        @pl.when(active(level))
        def _():
            for h in span:
                read_state(level, h)

        if level + 1 == bits:
            columns = slice(group * per * HD, (group + 1) * per * HD)
            att[core, :, columns] = acc[:, columns].astype(jnp.bfloat16)
            att_copy(group, True).start()

    own.wait()
    pair_landed().wait_recv()
    for part in range(len(orders)):
        at, source = source_of(part, (0,) * len(dims))
        forward(part, source, at, -1, "start")
        if not fused:
            forward(part, source, at, -1, "wait")
    loads[3].wait()

    def project(part):
        lo, size = cuts[part]
        columns = slice(lo, lo + size)
        flat = [wbuf[g, :, :, columns].reshape(-1, size) for g in range(2)]
        out_ref[:, columns] = jnp.dot(att[0], flat[0], preferred_element_type=jnp.float32) + jnp.dot(
            att[1], flat[1], preferred_element_type=jnp.float32
        )

    for event in events:
        if event[0] == "within":
            within_event(event[1])
        elif event[0] == "state":
            state_event(event[1], event[2])
        elif event[0] == "weight":
            weight_event(*event[1:])
        elif event[0] == "loop":
            lengths = [[dims[d][0] for d in order] for order in orders]

            def each(e, carry):
                for part, order in enumerate(orders):
                    for arrived in range(len(order)):
                        below = math.prod(lengths[part][:arrived])
                        ks = []
                        rest_e = e
                        for length in lengths[part]:
                            ks.append(rest_e % length)
                            rest_e = rest_e // length

                        @pl.when(jnp.logical_and(e >= below, e < below * lengths[part][arrived]))
                        def _():
                            weight_event(part, ks, arrived)

                return carry

            lax.fori_loop(1, n, each, 0)
        elif event[0] == "att":
            for group in range(groups):
                att_copy(group, False).wait_recv()
        elif event[0] == "project" and fused:
            project(event[1])

    def finish(part, e):
        ks = []
        for d in orders[part]:
            ks.append(e % dims[d][0])
            e = e // dims[d][0]
        return ks

    pair_copy().wait_send()
    for group in range(groups):
        att_copy(group, True).wait_send()
        for level in range(bits):
            @pl.when(sends(level))
            def _():
                state_copy(level, group).wait_send()
    if fused:
        for part in range(len(orders)):
            for e in range(n):
                ks = finish(part, e)
                at, source = source_of(part, ks)
                forward(part, source, at, arrived_by(ks), "wait")
    if not fused:
        stores = [pltpu.make_async_copy(att, att_hbm, load_sem.at[0]), pltpu.make_async_copy(wbuf, w_out_hbm, load_sem.at[1])]
        for store in stores:
            store.start()
        for store in stores:
            store.wait()


def schedule(dims, orders, cuts, n, heads, groups, unrolled):
    bits = n.bit_length() - 1
    whole = sum(size for _, size in cuts)
    timed = []
    for h in range(heads):
        timed.append((0.35 * h / heads, ("within", h)))
    for level in range(bits):
        for group in range(groups):
            timed.append((0.45 + 0.75 * level + 0.25 * group, ("state", level, group)))
    if not unrolled:
        tail = [("loop",), ("att",)]
    else:
        last = {}
        for part, order in enumerate(orders):
            lengths = [dims[d][0] for d in order]
            count = [0] * len(order)
            for rev in itertools.product(*[range(length) for length in lengths[::-1]]):
                ks = rev[::-1]
                arrived = max((r for r, k in enumerate(ks) if k), default=-1)
                if arrived < 0:
                    continue
                count[arrived] += 1
                when = count[arrived] * cuts[part][1] / whole * 1.8 + 0.3 * sum(1 for k in ks if k)
                if arrived == len(order) - 1 and lengths[-1] == 2:
                    when += 100
                timed.append((when, ("weight", part, ks, arrived)))
        tail = [("att",)]
    timed.sort(key=lambda t: t[0])
    return [e for _, e in timed] + tail + [("project", p) for p in range(len(orders))]


def planned_kernel(
    plan, q_hbm, k_hbm, v_hbm, pattern_ref, table_ref, w_hbm, out_ref,
    q_ref, k_ref, v_ref, w_ref, wbuf, att, acc, sub, outgoing, incoming, mixb,
    load_sem, own_sem, pair_send, pair_recv, w_send, w_recv, s_send, s_recv, a_send, a_recv,
):
    dims, parts, events, n = plan
    me = lax.axis_index("seq")
    core = lax.axis_index("head")
    other = 1 - core
    tokens, width = q_ref.shape
    rows = w_ref.shape[1]
    heads = width // HD
    cols = wbuf.shape[-1]
    bits = n.bit_length() - 1
    groups = s_recv.shape[1]
    per = heads // groups
    place = [me // stride % length for length, stride in dims]

    loads = {
        name: pltpu.make_async_copy(src, dst, load_sem.at[i])
        for i, (name, src, dst) in enumerate(
            (("w", w_hbm, w_ref), ("k", k_hbm, k_ref), ("v", v_hbm, v_ref), ("q", q_hbm, q_ref))
        )
    }
    for load in loads.values():
        load.start()

    barrier = pltpu.get_barrier_semaphore()
    total = 1
    pl.semaphore_signal(barrier, inc=1, device_id=(me, other), device_id_type=MESH)
    for (length, stride), p in zip(dims, place):
        for step in (-1, 1):
            there = jnp.logical_and(p + step >= 0, p + step < length)

            @pl.when(there)
            def _():
                for c in range(2):
                    pl.semaphore_signal(barrier, inc=1, device_id=(me + step * stride, c), device_id_type=MESH)

            total = total + 2 * there.astype(jnp.int32)
    for bit in range(bits - 1):
        if all(1 << bit != stride for _, stride in dims):
            pl.semaphore_signal(barrier, inc=1, device_id=(me ^ (1 << bit), core), device_id_type=MESH)
            total = total + 1

    waited = set()

    def loaded(*names):
        for name in names:
            if name not in waited:
                waited.add(name)
                loads[name].wait()

    loaded("w")
    pl.semaphore_wait(barrier, total)

    def head_cols(h):
        return slice(h * HD, (h + 1) * HD)

    def pair_copy(which):
        return pltpu.make_async_remote_copy(
            src_ref=w_ref.at[0, :, pl.ds(pl.multiple_of(other * cols, 128), cols)],
            dst_ref=wbuf.at[which, me], send_sem=pair_send, recv_sem=pair_recv,
            device_id=(me, other), device_id_type=MESH,
        )

    own = pltpu.make_async_copy(
        w_ref.at[0, :, pl.ds(pl.multiple_of(core * cols, 128), cols)], wbuf.at[core, me], own_sem
    )

    top = bits - 1
    reach, climb = dims[0]

    def state_copy(level, group, relay=False):
        piece = pl.ds(group * per, per)
        target = me + climb if level == top else me ^ (1 << level)
        return pltpu.make_async_remote_copy(
            src_ref=(incoming if relay else outgoing).at[level, piece], dst_ref=incoming.at[level, piece],
            send_sem=s_send.at[level], recv_sem=s_recv.at[level, group],
            device_id=(target, core), device_id_type=MESH,
        )

    def sum_needed(level, who=me):
        if level == top - 1:
            return who // climb == reach // 2 - 1
        return who // 2 ** (level + 1) != n // 2 ** (level + 1) - 1

    def active(level, who=me):
        return who // 2**level % 2 == 1

    def receives(level, who=me):
        if level == top:
            return active(level, who)
        return jnp.logical_or(active(level, who), sum_needed(level, who))

    def sends(level):
        if level == top:
            return place[0] == reach // 2 - 1
        return receives(level, me ^ (1 << level))

    relays = jnp.logical_and(active(top), place[0] < reach - 1)

    def first_copy(part, slot, target, half):
        g, lo, size, _ = parts[part]
        return pltpu.make_async_remote_copy(
            src_ref=w_ref.at[0, :, pl.ds(half * cols + lo, size)],
            dst_ref=wbuf.at[g, me, :, pl.ds(lo, size)],
            send_sem=w_send.at[part, slot], recv_sem=w_recv.at[part, me],
            device_id=(target, half), device_id_type=MESH,
        )

    def first(part, ranks):
        g, _, _, order = parts[part]
        for rank in ranks:
            d = order[rank]
            length, stride = dims[d]
            for slot, step in ((2 * rank, 1), (2 * rank + 1, -1)):
                ok = jnp.logical_and(place[d] + step >= 0, place[d] + step < length)

                @pl.when(jnp.logical_and(ok, core == g))
                def _():
                    for half in range(2):
                        first_copy(part, slot, me + step * stride, half).start()

    def weight_copy(part, source, slot, target):
        g, lo, size, _ = parts[part]
        piece = wbuf.at[g, source, :, pl.ds(lo, size)]
        return pltpu.make_async_remote_copy(
            src_ref=piece, dst_ref=piece,
            send_sem=w_send.at[part, slot], recv_sem=w_recv.at[part, source],
            device_id=(target, core), device_id_type=MESH,
        )

    def forward(part, ks):
        order = parts[part][3]
        at = {d: nearest(k, place[d], dims[d][0]) for d, k in zip(order, ks)}
        source = sum(at[d] * dims[d][1] for d in at)
        arrived = max(r for r, k in enumerate(ks) if k)
        weight_copy(part, source, 0, me).wait_recv()
        for rank in range(arrived, len(order)):
            d = order[rank]
            length, stride = dims[d]
            for slot, step in ((2 * rank, 1), (2 * rank + 1, -1)):
                if rank == arrived and length == 2:
                    continue
                ok = jnp.logical_and(place[d] + step >= 0, place[d] + step < length)
                if rank == arrived:
                    ok = jnp.logical_and(ok, (place[d] - at[d]) * step > 0)

                @pl.when(ok)
                def _():
                    weight_copy(part, source, slot, me + step * stride).start()

    def sent(part):
        g, lo, size, order = parts[part]
        ahead = 1
        for rank, d in enumerate(order):
            length = dims[d][0]
            for slot, up in ((2 * rank, True), (2 * rank + 1, False)):
                for p in range(length - 1) if up else range(1, length):
                    count = ahead - 1 + ahead * (p if up else length - 1 - p)
                    for mine in (0, 2):
                        if count + mine == 0:
                            continue

                        @pl.when(jnp.logical_and(place[d] == p, (core == g) == (mine == 2)))
                        def _():
                            piece = wbuf.at[g, pl.ds(0, count + mine), :, pl.ds(lo, size)]
                            pltpu.make_async_remote_copy(
                                src_ref=piece, dst_ref=piece, send_sem=w_send.at[part, slot], recv_sem=w_recv.at[part, 0],
                                device_id=(me, other), device_id_type=MESH,
                            ).wait_send()

            ahead *= length

    def make_mix():
        ids = lax.broadcasted_iota(jnp.int32, (table_ref.shape[0], tokens), 0)
        one_hot = (ids == pattern_ref[...].reshape(1, tokens)).astype(jnp.float32)
        mix = lax.dot_general(
            one_hot, table_ref[...], (((0,), (0,)), ((), ())),
            precision=lax.Precision.HIGHEST, preferred_element_type=jnp.float32,
        )
        for l in range(bits + 1):
            factor = 1.0 / math.sqrt(tokens * (1 if l == 0 else 2 ** (l - 1)))
            mixb[l] = jnp.broadcast_to(mix[:, l : l + 1] * factor, (tokens, HD))

    def state_start(group):
        loaded("k", "v")
        for h in range(group * per, (group + 1) * per):
            state = lax.dot_general(
                k_ref[:, head_cols(h)], v_ref[:, head_cols(h)], (((0,), (0,)), ((), ())),
                preferred_element_type=jnp.float32,
            )
            sub[h] = state
            outgoing[0, h] = state.astype(jnp.bfloat16)

        @pl.when(sends(0))
        def _():
            state_copy(0, group).start()

    def within_event(h):
        columns = head_cols(h)
        scores = lax.dot_general(
            q_ref[:, columns], k_ref[:, columns], (((1,), (1,)), ((), ())),
            preferred_element_type=jnp.float32,
        )
        row = lax.broadcasted_iota(jnp.int32, (tokens, tokens), 0)
        col = lax.broadcasted_iota(jnp.int32, (tokens, tokens), 1)
        inner = jnp.where(col <= row, scores, 0.0).astype(jnp.bfloat16)
        acc[:, columns] = mixb[0] * jnp.dot(inner, v_ref[:, columns], preferred_element_type=jnp.float32)

    def att_copy(group):
        columns = pl.ds(group * per * HD, per * HD)
        return pltpu.make_async_remote_copy(
            src_ref=att.at[core, :, columns], dst_ref=att.at[core, :, columns],
            send_sem=a_send, recv_sem=a_recv,
            device_id=(me, other), device_id_type=MESH,
        )

    def att_whole(which):
        return pltpu.make_async_remote_copy(
            src_ref=att.at[which], dst_ref=att.at[which], send_sem=a_send, recv_sem=a_recv,
            device_id=(me, other), device_id_type=MESH,
        )

    def state_event(level, group):
        @pl.when(receives(level))
        def _():
            state_copy(level, group).wait_recv()

        span = range(group * per, (group + 1) * per)
        if level + 1 < bits:
            @pl.when(sum_needed(level))
            def _():
                for h in span:
                    summed = sub[h] + incoming[level, h].astype(jnp.float32)
                    sub[h] = summed
                    outgoing[level + 1, h] = summed.astype(jnp.bfloat16)

            @pl.when(sends(level + 1))
            def _():
                state_copy(level + 1, group).start()
        else:
            @pl.when(relays)
            def _():
                state_copy(level, group, True).start()

    def read_event(level, group):
        @pl.when(active(level))
        def _():
            for h in range(group * per, (group + 1) * per):
                acc[:, head_cols(h)] += mixb[level + 1] * jnp.dot(
                    q_ref[:, head_cols(h)], incoming[level, h], preferred_element_type=jnp.float32
                )

        if level + 1 == bits:
            columns = slice(group * per * HD, (group + 1) * per * HD)
            att[core, :, columns] = acc[:, columns].astype(jnp.bfloat16)
            att_copy(group).start()

    def project(part, k):
        g, lo, size, _ = parts[part]
        length, stride = dims[0]
        slab = nearest(k, place[0], length) * stride
        depth = stride * rows
        piece = wbuf[g, pl.ds(slab, stride), :, lo : lo + size].reshape(depth, size)
        taken = att[g, :, pl.ds(pl.multiple_of(slab * rows, math.gcd(depth, 1024)), depth)]
        out_ref[:, lo : lo + size] += jnp.dot(taken, piece, preferred_element_type=jnp.float32)

    for event in events:
        kind, args = event[0], event[1:]
        if kind == "first":
            first(*args)
        elif kind == "pair":
            pair_copy(core).start()
            own.start()
        elif kind == "paired":
            own.wait()
            pair_copy(other).wait_recv()
        elif kind == "start":
            state_start(*args)
        elif kind == "mix":
            make_mix()
            out_ref[...] = jnp.zeros_like(out_ref)
        elif kind == "within":
            loaded("k", "v", "q")
            within_event(*args)
        elif kind == "state":
            state_event(*args)
        elif kind == "read":
            read_event(*args)
        elif kind == "weight":
            forward(*args)
        elif kind == "att":
            att_whole(other).wait_recv()
        elif kind == "project":
            project(*args)

    pair_copy(core).wait_send()
    att_whole(core).wait_send()
    for level in range(bits):
        @pl.when(jnp.logical_or(sends(level), relays) if level == top else sends(level))
        def _():
            pltpu.make_async_remote_copy(
                src_ref=outgoing.at[level], dst_ref=incoming.at[level],
                send_sem=s_send.at[level], recv_sem=s_recv.at[level, 0],
                device_id=(me ^ (1 << level), core), device_id_type=MESH,
            ).wait_send()
    for part in range(len(parts)):
        sent(part)


def make_parts(dims, tiles):
    long = max(range(3), key=lambda i: dims[i][0])
    a, b = [i for i in range(3) if i != long]
    direct = max(1, tiles // 8)
    most = (tiles - direct + 1) // 2
    parts = []
    for g, sizes in enumerate(((most, tiles - direct - most, direct), (tiles - direct - most, most, direct))):
        last = (b, a, long) if g == 0 else (a, b, long)
        lo = 0
        for size, order in zip(sizes, ((long, b, a), (long, a, b), last)):
            parts.append((g, lo * 128, size * 128, order))
            lo += size
    return parts


def make_events(dims, parts, n, heads, groups):
    bits = n.bit_length() - 1
    timed = []
    for part, (_, _, _, order) in enumerate(parts):
        for rank, d in enumerate(order):
            timed.append(((0, rank, part), ("first", part, (rank,))))
    for group in range(groups):
        timed.append(((1, group), ("start", group)))
    for h in range(heads):
        timed.append(((3 + h, 9), ("within", h)))
    for level in range(bits):
        for group in range(groups):
            timed.append(((3 + 3 * level + group, 0), ("state", level, group)))
    for part, (_, _, _, order) in enumerate(parts):
        for ks in itertools.product(*[range(dims[d][0]) for d in order]):
            if any(ks):
                timed.append(((3 * sum(1 for k in ks if k) + sum(ks), part), ("weight", part, ks)))
    if ORDER and len(ORDER) == len(timed) and [d[0] for d in dims] == LENGTHS:
        chosen = [timed[i][1] for i in ORDER]
    else:
        chosen = [event for _, event in sorted(timed, key=lambda t: t[0])]
    events, inside = [], []
    for event in chosen:
        if event[0] == "within" and event[1] in inside:
            continue
        due = [event[1]] if event[0] == "within" else []
        if event[0] == "state":
            events.append(event)
            per = heads // groups
            due = [h for h in range(event[2] * per, (event[2] + 1) * per) if h not in inside]
        if due and not inside:
            events.append(("mix",))
        events += [("within", h) for h in due]
        inside += due
        if event[0] == "state":
            events.append(("read",) + event[1:])
        elif event[0] != "within":
            events.append(event)
    at = 1 + max(i for i, e in enumerate(events) if e[0] == "start")
    events.insert(at, ("pair",))
    reads = max(i for i, e in enumerate(events) if e[0] == "read")
    at = min(len(events), reads + 1 + LAG)
    events[at:at] = [("paired",), ("att",)]
    ready = {}
    for i, e in enumerate(events):
        if e[0] == "weight":
            key = (e[1], e[2][parts[e[1]][3].index(0)])
            ready[key] = max(ready.get(key, at + 1), i)
    placed, queue = [], []
    for i, e in enumerate(events):
        placed.append(e)
        queue += sorted((key for key, j in ready.items() if j == i), key=lambda key: key[::-1])
        if queue and i + 1 < len(events):
            placed.append(("project",) + queue.pop(0))
    placed += [("project",) + key for key in queue]
    return placed


def planned(dims, queries, keys, values, level_pattern, level_weight, out_weight):
    n = lax.axis_size("seq")
    tokens, width = queries.shape
    heads = width // HD
    bits = n.bit_length() - 1
    _, rows, full = out_weight.shape
    cols = full // 2
    groups = min(4, heads)
    parts = make_parts(dims, cols // 128)
    events = make_events(dims, parts, n, heads, groups)
    bf16, f32 = jnp.bfloat16, jnp.float32
    any_spec = pl.BlockSpec(memory_space=pl.ANY)
    vmem_spec = pl.BlockSpec(memory_space=pltpu.VMEM)
    dma = pltpu.SemaphoreType.DMA
    return pl.pallas_call(
        functools.partial(planned_kernel, (dims, parts, events, n)),
        out_shape=pltpu.VMEM((tokens, cols), f32),
        in_specs=[any_spec] * 3 + [vmem_spec] * 2 + [any_spec],
        out_specs=vmem_spec,
        scratch_shapes=[
            pltpu.VMEM((tokens, width), bf16),
            pltpu.VMEM((tokens, width), bf16),
            pltpu.VMEM((tokens, width), bf16),
            pltpu.VMEM((1, rows, full), bf16),
            pltpu.VMEM((2, n, rows, cols), bf16),
            pltpu.VMEM((2, tokens, width), bf16),
            pltpu.VMEM((tokens, width), f32),
            pltpu.VMEM((heads, HD, HD), f32),
            pltpu.VMEM((bits, heads, HD, HD), bf16),
            pltpu.VMEM((bits, heads, HD, HD), bf16),
            pltpu.VMEM((bits + 1, tokens, HD), f32),
            dma((4,)),
            dma,
            dma,
            dma,
            dma((len(parts), 2 * len(dims))),
            dma((len(parts), n)),
            dma((bits,)),
            dma((bits, groups)),
            dma,
            dma,
        ],
        compiler_params=pltpu.CompilerParams(
            collective_id=0, has_side_effects=True, vmem_limit_bytes=60 * 2**20
        ),
    )(queries, keys, values, level_pattern, level_weight, out_weight)


def on_device(dims, queries, keys, values, level_pattern, level_weight, out_weight):
    n = lax.axis_size("seq")
    tokens, width = queries.shape
    heads = width // HD
    bits = n.bit_length() - 1
    _, rows, full = out_weight.shape
    cols = full // 2
    fused = rows % 16 == 0
    if fused and len(dims) == 3 and cols % 1024 == 0:
        return planned(dims, queries, keys, values, level_pattern, level_weight, out_weight)
    groups = min(4, heads)
    tiles = cols // 128
    if len(dims) == 3:
        long = max(range(3), key=lambda i: dims[i][0])
        a, b = [i for i in range(3) if i != long]
        orders = [(long, a, b), (long, b, a), (a, b, long)]
        share = max(1, tiles * 3 // 8)
        sizes = [share, share, tiles - 2 * share]
    else:
        orders, sizes = [tuple(range(len(dims)))], [tiles]
    cuts, lo = [], 0
    for size in sizes:
        cuts.append((lo * 128, size * 128))
        lo += size
    events = schedule(dims, orders, cuts, n, heads, groups, fused)
    plan = (dims, orders, cuts, events, n, fused)
    bf16, f32 = jnp.bfloat16, jnp.float32
    any_spec = pl.BlockSpec(memory_space=pl.ANY)
    vmem_spec = pl.BlockSpec(memory_space=pltpu.VMEM)
    if fused:
        out_shape = pltpu.VMEM((tokens, cols), f32)
        out_specs = vmem_spec
    else:
        out_shape = [
            jax.ShapeDtypeStruct((2, tokens, width), bf16),
            jax.ShapeDtypeStruct((2, n, rows, cols), bf16),
        ]
        out_specs = [any_spec, any_spec]
    dma = pltpu.SemaphoreType.DMA
    result = pl.pallas_call(
        functools.partial(kernel, plan),
        out_shape=out_shape,
        in_specs=[any_spec] * 3 + [vmem_spec] * 2 + [any_spec],
        out_specs=out_specs,
        scratch_shapes=[
            pltpu.VMEM((tokens, width), bf16),
            pltpu.VMEM((tokens, width), bf16),
            pltpu.VMEM((tokens, width), bf16),
            pltpu.VMEM((1, rows, full), bf16),
            pltpu.VMEM((2, n, rows, cols), bf16),
            pltpu.VMEM((2, tokens, width), bf16),
            pltpu.VMEM((tokens, width), f32),
            pltpu.VMEM((heads, HD, HD), f32),
            pltpu.VMEM((bits, heads, HD, HD), bf16),
            pltpu.VMEM((bits, heads, HD, HD), bf16),
            pltpu.VMEM((bits + 1, tokens, HD), f32),
            dma((4,)),
            dma,
            dma,
            dma,
            dma((len(orders), n if fused else 1, 2 * len(dims))),
            dma((len(orders), n)),
            dma((bits, groups)),
            dma((bits, groups)),
            dma((groups,)),
            dma((groups,)),
        ],
        compiler_params=pltpu.CompilerParams(
            collective_id=0, has_side_effects=True, vmem_limit_bytes=60 * 2**20
        ),
    )(queries, keys, values, level_pattern, level_weight, out_weight)
    if fused:
        return result
    att, gathered = result
    return jnp.einsum(
        "gtk,gkd->td", att, gathered.reshape(2, n * rows, cols), preferred_element_type=f32
    )


def solution(mesh):
    placed = (
        P("seq", "head"),
        P("seq", "head"),
        P("seq", "head"),
        P("seq"),
        P(),
        P("head", "seq", None),
    )
    return jax.shard_map(
        functools.partial(on_device, line_dims(mesh)),
        mesh=mesh, in_specs=placed, out_specs=P("seq", "head"), check_vma=False,
    )
```
